32 devices in a mesh: tm: 4 (over y, x), space: 8 (over z, core).
Axes of the slice: x: 2, y: 2, z: 4, core: 2. Of those that a mesh axis runs over, the one named last changes fastest.
Arguments:
- snapshots: bfloat16 [128, 256, 8192], P('tm', None, 'space'), may hold values from -6 to 6
- weights: float32 [8192], P('space'), may hold values from 6.1035156e-05 to 0.0009765625
Outputs:
- spectra: float32 [128, 128, 2, 128], P('space', 'tm')
The draws below stay inside these ranges and needn't reach their ends.
All inputs are finite; a program needn't handle non-finite values.
Results may differ from the reference program's by a relative error of at most 0.0027.
Values may be sent and summed in bfloat16 or wider, within the bound.
A program may use at most 192 MiB of HBM per device.

```python
import math
import jax
import jax.numpy as jnp
from jax import lax

NB = 128
NFFT = 256
NF = 128
X_DEV = 1024
XTOT = 8192
N_SPACE = 8


def shard_levels(key, dims, split, low, high):
    loudness, own = 1.0, jax.random.fold_in(key, 6)
    for position, parts in split:
        draws = jnp.exp(jax.random.uniform(jax.random.fold_in(own, position), (parts,), jnp.float32, low / len(split), high / len(split)))
        loudness = loudness * jnp.repeat(draws, dims[position] // parts).reshape([-1 if axis == position else 1 for axis in range(len(dims))])
    return loudness


def noise(own_key, shape, spread, limit, split=(), kind=jnp.bfloat16):
    result = jax.random.normal(own_key, shape, jnp.float32) * spread
    if len(split) > 0:
        result = shard_levels(own_key, shape, split, -0.22, 0.18) * result
    return jnp.clip(result, min=-limit, max=limit).astype(kind)


def setup_inputs(seed: int = 0) -> dict:
    key_of = jax.random.split(jax.random.key(seed), 3)
    snapshots = noise(key_of[0], (NB, NFFT, XTOT), 1.0, 6.0, ((0, 4), (2, 8)))
    weights = jnp.clip(jnp.exp(math.log(0.0009765625) - 2.7725887 * jax.random.uniform(key_of[1], (XTOT,), jnp.float32) ** shard_levels(key_of[1], (XTOT,), ((0, 8),), -0.2, 0.2)), 6.103515625e-05, 0.0009765625)
    return dict(snapshots=snapshots, weights=weights)


def make_table():
    steps_t = jnp.arange(NFFT, dtype=jnp.int32)
    freqs = jnp.arange(NF, dtype=jnp.int32)
    phase = (freqs[:, None] * steps_t[None, :] % NFFT).astype(jnp.float32) * (2.0 * math.pi / NFFT)
    hann = 0.5 - 0.5 * jnp.cos(steps_t.astype(jnp.float32) * (2.0 * math.pi / NFFT))
    factor = 1.0 / math.sqrt(3.0 * NFFT / 8.0)
    table = jnp.concatenate([jnp.cos(phase), -jnp.sin(phase)], axis=0) * hann[None, :] * factor
    return table.astype(jnp.bfloat16)

def reference(snapshots, weights):
    table = make_table().astype(jnp.float32)
    highest = lax.Precision.HIGHEST

    def accumulate(index, total):
        start = index * X_DEV
        block = lax.dynamic_slice_in_dim(snapshots, start, X_DEV, 2).astype(jnp.float32)
        scale = jnp.sqrt(lax.dynamic_slice_in_dim(weights, start, X_DEV, 0))
        coeffs = jnp.einsum('kt,btx->bkx', table, block, precision=highest) * scale[None, None, :]
        coeffs = coeffs.reshape(NB, 2, NF, X_DEV)
        real_part = jnp.einsum('acfx,bcfx->afb', coeffs, coeffs, precision=highest)
        imag_part = jnp.einsum('afx,bfx->afb', coeffs[:, 0], coeffs[:, 1], precision=highest) - jnp.einsum('afx,bfx->afb', coeffs[:, 1], coeffs[:, 0], precision=highest)
        return total + jnp.stack([real_part, imag_part], axis=2)
    start_total = jnp.zeros((NB, NF, 2, NB), jnp.float32)
    return lax.fori_loop(0, N_SPACE, accumulate, start_total)
```

```python
import functools
import math

import jax
import jax.numpy as jnp
import numpy as np
from jax import lax
from jax.experimental import pallas as pl
from jax.experimental.pallas import tpu as pltpu
from jax.sharding import PartitionSpec as P

MESH = pl.DeviceIdType.MESH
WIDTH = 128
GROUP = 16


def make_table(length, count):
    steps_t = np.arange(length, dtype=np.int32)
    freqs = np.arange(count, dtype=np.int32)
    turn = np.float32(2.0 * math.pi / length)
    phase = (freqs[:, None] * steps_t[None, :] % length).astype(np.float32) * turn
    hann = np.float32(0.5) - np.float32(0.5) * np.cos(steps_t.astype(np.float32) * turn)
    factor = np.float32(1.0 / math.sqrt(3.0 * length / 8.0))
    table = np.concatenate([np.cos(phase), -np.sin(phase)], axis=0) * hann[None, :] * factor
    return jnp.asarray(table.astype(jnp.bfloat16))


def swap_matrix():
    size = GROUP * GROUP
    source = np.arange(size).reshape(GROUP, GROUP).T.reshape(-1)
    return jnp.asarray(np.eye(size, dtype=np.float32)[source].astype(jnp.bfloat16))


def order_matrix(unit_size, blocks, n_space):
    size = unit_size * 2 * blocks
    rows = blocks // n_space
    source = np.arange(size).reshape(unit_size, 2, n_space, rows).transpose(2, 0, 1, 3).reshape(-1)
    return jnp.asarray(np.eye(size, dtype=np.float32)[source].astype(jnp.bfloat16))


def partner(me, k, count):
    if count & (count - 1):
        return lax.rem(me + k, count)
    other, bit = 0, 1
    while bit < count:
        have = lax.rem(lax.div(me, bit), 2)
        other = other + bit * (1 - have if k & bit else have)
        bit *= 2
    return other


def hops(k, count):
    return 1 if count & (count - 1) else bin(k).count("1")


def meetings(n_tm, n_space):
    return max(n_space // 2, max(hops(k, n_tm) for k in range(1, n_tm)))


def kernel(
    n_tm, n_space, width, early, unit_size, later,
    x_ref, w_hbm, table_hbm, swap_hbm, order_hbm, out_buf,
    w_ref, table_ref, swap_ref, order_ref,
    x_buf, rows_buf, outgoing, owned, part, arrived,
    const_sem, x_sem, early_send, early_recv, unit_send, unit_recv, sum_send, sum_recv, round_sem,
):
    me = lax.axis_index("tm")
    seat = lax.axis_index("space")
    blocks, length, points = x_ref.shape
    half = length // 2
    freqs = half // n_tm
    tiles = points // width
    steps = blocks // GROUP * tiles
    units = freqs // unit_size
    total = blocks * n_tm
    rows = total // n_space
    slab = unit_size * 2 * rows
    near = [k for k in range(1, n_tm) if hops(k, n_tm) == 1]
    far = [k for k in range(1, n_tm) if hops(k, n_tm) > 1]
    peers = near + far
    tm_rounds = max(hops(k, n_tm) for k in peers)
    rounds = meetings(n_tm, n_space)
    seats = list(range(n_space - 1, 0, -1))

    def place(step):
        start = pl.multiple_of(step // tiles * GROUP, GROUP)
        return start, pl.multiple_of(step % tiles * width, width)

    def load(step):
        start, column = place(step)
        return pltpu.make_async_copy(
            x_ref.at[pl.ds(start, GROUP), :, pl.ds(column, width)],
            x_buf.at[step % 2],
            x_sem.at[step % 2],
        )

    def early_copy(step, k):
        start, column = place(step)
        return pltpu.make_async_remote_copy(
            src_ref=outgoing.at[k - 1, pl.ds(0, early), :, pl.ds(start, GROUP), pl.ds(column, width)],
            dst_ref=owned.at[
                pl.ds(0, early), :, pl.ds(pl.multiple_of(me * blocks + start, GROUP), GROUP), pl.ds(column, width)
            ],
            send_sem=early_send.at[step, k - 1],
            recv_sem=early_recv.at[step, k - 1],
            device_id={"tm": partner(me, k, n_tm)},
            device_id_type=MESH,
        )

    def later_copy(item, k):
        first, size, column, span = later[item]
        columns = pl.ds(column, span)
        return pltpu.make_async_remote_copy(
            src_ref=outgoing.at[k - 1, pl.ds(first, size), :, :, columns],
            dst_ref=owned.at[pl.ds(first, size), :, pl.ds(pl.multiple_of(me * blocks, GROUP), blocks), columns],
            send_sem=unit_send.at[item, k - 1],
            recv_sem=unit_recv.at[item, k - 1],
            device_id={"tm": partner(me, k, n_tm)},
            device_id_type=MESH,
        )

    def sum_copy(unit, k):
        owner = partner(seat, k, n_space)
        return pltpu.make_async_remote_copy(
            src_ref=part.at[unit, owner],
            dst_ref=arrived.at[unit, k - 1],
            send_sem=sum_send.at[unit],
            recv_sem=sum_recv.at[unit],
            device_id={"space": owner},
            device_id_type=MESH,
        )

    constants = [
        pltpu.make_async_copy(pair[0], pair[1], const_sem.at[i])
        for i, pair in enumerate(
            [(table_hbm, table_ref), (w_hbm, w_ref), (swap_hbm, swap_ref), (order_hbm, order_ref)]
        )
    ]
    constants[0].start()
    constants[1].start()
    load(0).start()
    constants[2].start()
    constants[3].start()
    barrier = pltpu.get_barrier_semaphore()
    core = seat + 1 - 2 * lax.rem(seat, 2)
    met = len(near) + 1 + (seat >= 2).astype(jnp.int32) + (seat + 2 < n_space).astype(jnp.int32)

    def greet(semaphore):
        for k in near:
            pl.semaphore_signal(semaphore, inc=1, device_id={"tm": partner(me, k, n_tm)}, device_id_type=MESH)
        pl.semaphore_signal(semaphore, inc=1, device_id={"space": core}, device_id_type=MESH)

        @pl.when(seat >= 2)
        def _():
            pl.semaphore_signal(semaphore, inc=1, device_id={"space": seat - 2}, device_id_type=MESH)

        @pl.when(seat + 2 < n_space)
        def _():
            pl.semaphore_signal(semaphore, inc=1, device_id={"space": seat + 2}, device_id_type=MESH)

    greet(barrier)
    for copy in constants:
        copy.wait()

    def transform(step, carry):
        start, column = place(step)

        @pl.when(step + 1 < steps)
        def _():
            load(step + 1).start()

        load(step).wait()
        scale = jnp.sqrt(w_ref[:, pl.ds(column, width)])

        def one(b, inner):
            product = jnp.dot(table_ref[...], x_buf[step % 2, b], preferred_element_type=jnp.float32)
            rows_buf[b] = (product * scale).astype(jnp.bfloat16)
            return inner

        lax.fori_loop(0, GROUP, one, 0, unroll=2)
        def exchange(k, f):
            target = owned if k == 0 else outgoing.at[k - 1]
            base = partner(me, k, n_tm) * freqs
            offset = me * blocks + start if k == 0 else start
            for c in range(2):
                row = pl.multiple_of(c * half + base + f, GROUP)
                taken = rows_buf[:, pl.ds(row, GROUP), :].reshape(GROUP * GROUP, width)
                swapped = jnp.dot(swap_ref[...], taken, preferred_element_type=jnp.float32)
                target[
                    pl.ds(f, GROUP), c, pl.ds(pl.multiple_of(offset, GROUP), GROUP), pl.ds(column, width)
                ] = swapped.astype(jnp.bfloat16).reshape(GROUP, GROUP, width)

        starts = range(0, freqs, GROUP)
        for k in near:
            for f in starts:
                if f < early:
                    exchange(k, f)

        @pl.when(step == 0)
        def _():
            pl.semaphore_wait(barrier, met)
            if rounds > 1:
                greet(round_sem.at[0])

        for k in near:
            early_copy(step, k).start()
        for k in far:
            for f in starts:
                if f < early:
                    exchange(k, f)
        for k in peers:
            for f in starts:
                if f >= early:
                    exchange(k, f)
        for f in starts:
            exchange(0, f)

        @pl.when(step == 0)
        def _():
            for r in range(1, tm_rounds):
                pl.semaphore_wait(round_sem.at[r - 1], met)
                if r + 1 < rounds:
                    greet(round_sem.at[r])

        for k in far:
            early_copy(step, k).start()
        return carry

    lax.fori_loop(0, steps, transform, 0)

    for item in range(len(later)):
        for k in peers:
            later_copy(item, k).start()

    def meet(r, carry):
        pl.semaphore_wait(round_sem.at[r - 1], met)

        @pl.when(r + 1 < rounds)
        def _():
            greet(round_sem.at[r])

        return carry

    lax.fori_loop(tm_rounds, rounds, meet, 0)

    def early_wait(step, carry):
        for k in range(1, n_tm):
            early_copy(step, k).wait()
        return carry

    lax.fori_loop(0, steps, early_wait, 0)

    def finish(unit):
        pltpu.make_async_copy(arrived.at[unit], arrived.at[unit], sum_recv.at[unit]).wait()
        value = part[unit, seat].astype(jnp.float32)
        for k in range(n_space - 1):
            value = value + arrived[unit, k].astype(jnp.float32)
        for i in range(2 * unit_size):
            out_buf[:, pl.ds(unit * 2 * unit_size + i, 1), :] = value[i * rows : (i + 1) * rows][:, None, :]

    def cross(unit, carry):
        for item in range(len(later) - 1):

            @pl.when(unit == later[item][0] // unit_size)
            def _(item=item):
                for k in peers:
                    later_copy(item, k).wait_recv()

        pieces = []
        grams = []
        for column in (0, points // 2):
            if column:

                @pl.when(unit == units - 1)
                def _():
                    for k in peers:
                        later_copy(len(later) - 1, k).wait_recv()

            for i in range(unit_size):
                both = owned[unit * unit_size + i, :, :, pl.ds(column, points // 2)]
                both = both.reshape(2 * total, points // 2)
                grams.append(
                    lax.dot_general(both, both, (((1,), (1,)), ((), ())), preferred_element_type=jnp.float32)
                )
        for i in range(unit_size):
            gram = grams[i] + grams[unit_size + i]
            pieces.append(gram[:total, :total] + gram[total:, total:])
            pieces.append(gram[:total, total:] - gram[total:, :total])
        pieces = [piece.astype(jnp.bfloat16) for piece in pieces]
        if rows % GROUP == 0:
            for i, piece in enumerate(pieces):
                for d in range(n_space):
                    part[unit, d, i * rows : (i + 1) * rows, :] = piece[d * rows : (d + 1) * rows]
        else:
            ordered = jnp.dot(
                order_ref[...], jnp.concatenate(pieces, axis=0), preferred_element_type=jnp.float32
            )
            part[unit] = ordered.astype(jnp.bfloat16).reshape(n_space, slab, total)

        for k in seats:
            sum_copy(unit, k).start()

        @pl.when(unit > 1)
        def _():
            finish(unit - 2)

        return carry

    lax.fori_loop(0, units, cross, 0)
    for unit in (units - 2, units - 1):
        finish(unit)

    def sent(unit, carry):
        pltpu.make_async_copy(arrived.at[unit], arrived.at[unit], sum_send.at[unit]).wait()
        return carry

    lax.fori_loop(0, units, sent, 0)
    for item in range(len(later)):
        for k in peers:
            later_copy(item, k).wait_send()


def per_device(n_tm, n_space, snapshots, weights):
    blocks, length, points = snapshots.shape
    total, freqs = blocks * n_tm, length // 2 // n_tm
    rows = total // n_space
    unit_size = max(1, GROUP // (2 * rows))
    units = freqs // unit_size
    slab = unit_size * 2 * rows
    width = min(WIDTH, points)
    early = max(freqs // 4, unit_size)
    later, first = [], early
    while first + unit_size < freqs:
        size = max(unit_size, (freqs - first) // (2 * unit_size) * unit_size)
        later.append((first, size, 0, points))
        first += size
    later += [(first, unit_size, column, points // 2) for column in (0, points // 2)]
    steps = blocks // GROUP * (points // width)
    hbm = pl.BlockSpec(memory_space=pl.ANY)
    bf16 = jnp.bfloat16
    table = make_table(length, length // 2)
    swap = swap_matrix()
    order = swap if rows % GROUP == 0 else order_matrix(unit_size, total, n_space)
    sums = pl.pallas_call(
        functools.partial(kernel, n_tm, n_space, width, early, unit_size, later),
        out_shape=jax.ShapeDtypeStruct((rows, freqs * 2, total), jnp.float32),
        in_specs=[hbm] * 5,
        out_specs=pl.BlockSpec(memory_space=pltpu.VMEM),
        scratch_shapes=[
            pltpu.VMEM((1, points), jnp.float32),
            pltpu.VMEM(table.shape, bf16),
            pltpu.VMEM(swap.shape, bf16),
            pltpu.VMEM(order.shape, bf16),
            pltpu.VMEM((2, GROUP, length, width), bf16),
            pltpu.VMEM((GROUP, length, width), bf16),
            pltpu.VMEM((n_tm - 1, freqs, 2, blocks, points), bf16),
            pltpu.VMEM((freqs, 2, total, points), bf16),
            pltpu.VMEM((units, n_space, slab, total), bf16),
            pltpu.VMEM((units, n_space - 1, slab, total), bf16),
            pltpu.SemaphoreType.DMA((4,)),
            pltpu.SemaphoreType.DMA((2,)),
            pltpu.SemaphoreType.DMA((steps, n_tm - 1)),
            pltpu.SemaphoreType.DMA((steps, n_tm - 1)),
            pltpu.SemaphoreType.DMA((len(later), n_tm - 1)),
            pltpu.SemaphoreType.DMA((len(later), n_tm - 1)),
            pltpu.SemaphoreType.DMA((units,)),
            pltpu.SemaphoreType.DMA((units,)),
            pltpu.SemaphoreType.REGULAR((max(meetings(n_tm, n_space) - 1, 1),)),
        ],
        compiler_params=pltpu.CompilerParams(
            collective_id=0, has_side_effects=True, vmem_limit_bytes=60 * 1024 * 1024
        ),
    )(
        snapshots,
        weights[None, :],
        table,
        swap,
        order,
    )
    return sums.reshape(rows, freqs, 2, total)


def solution(mesh):
    return jax.shard_map(
        functools.partial(per_device, mesh.shape["tm"], mesh.shape["space"]),
        mesh=mesh,
        in_specs=(P("tm", None, "space"), P("space")),
        out_specs=P("space", "tm", None, None),
        check_vma=False,
    )
```

```python
import functools
import math

import jax
import jax.numpy as jnp
import numpy as np
from jax import lax
from jax.experimental import pallas as pl
from jax.experimental.pallas import tpu as pltpu
from jax.sharding import PartitionSpec as P

MESH = pl.DeviceIdType.MESH
WIDTH = 128
GROUP = 16


def make_table(length, count):
    steps_t = np.arange(length, dtype=np.int32)
    freqs = np.arange(count, dtype=np.int32)
    turn = np.float32(2.0 * math.pi / length)
    phase = (freqs[:, None] * steps_t[None, :] % length).astype(np.float32) * turn
    hann = np.float32(0.5) - np.float32(0.5) * np.cos(steps_t.astype(np.float32) * turn)
    factor = np.float32(1.0 / math.sqrt(3.0 * length / 8.0))
    table = np.concatenate([np.cos(phase), -np.sin(phase)], axis=0) * hann[None, :] * factor
    return jnp.asarray(table.astype(jnp.bfloat16))


def swap_matrix():
    size = GROUP * GROUP
    source = np.arange(size).reshape(GROUP, GROUP).T.reshape(-1)
    return jnp.asarray(np.eye(size, dtype=np.float32)[source].astype(jnp.bfloat16))


def order_matrix(unit_size, blocks, n_space):
    size = unit_size * 2 * blocks
    rows = blocks // n_space
    source = np.arange(size).reshape(unit_size, 2, n_space, rows).transpose(2, 0, 1, 3).reshape(-1)
    return jnp.asarray(np.eye(size, dtype=np.float32)[source].astype(jnp.bfloat16))


def partner(me, k, count):
    if count & (count - 1):
        return lax.rem(me + k, count)
    other, bit = 0, 1
    while bit < count:
        have = lax.rem(lax.div(me, bit), 2)
        other = other + bit * (1 - have if k & bit else have)
        bit *= 2
    return other


def kernel(
    n_tm, n_space, width, early, unit_size, later,
    x_ref, w_hbm, table_hbm, swap_hbm, order_hbm, out_buf,
    w_ref, table_ref, swap_ref, order_ref,
    x_buf, rows_buf, outgoing, owned, part, arrived,
    const_sem, x_sem, early_send, early_recv, unit_send, unit_recv, sum_send, sum_recv, round_sem,
):
    me = lax.axis_index("tm")
    seat = lax.axis_index("space")
    blocks, length, points = x_ref.shape
    half = length // 2
    freqs = half // n_tm
    tiles = points // width
    steps = blocks // GROUP * tiles
    units = freqs // unit_size
    total = blocks * n_tm
    rows = total // n_space
    slab = unit_size * 2 * rows
    peers = list(range(n_tm - 1, 0, -1))
    rounds = n_space // 2
    seats = list(range(n_space - 1, 0, -1))

    def place(step):
        start = pl.multiple_of(step // tiles * GROUP, GROUP)
        return start, pl.multiple_of(step % tiles * width, width)

    def load(step):
        start, column = place(step)
        return pltpu.make_async_copy(
            x_ref.at[pl.ds(start, GROUP), :, pl.ds(column, width)],
            x_buf.at[step % 2],
            x_sem.at[step % 2],
        )

    def early_copy(step, k):
        start, column = place(step)
        return pltpu.make_async_remote_copy(
            src_ref=outgoing.at[k - 1, pl.ds(0, early), :, pl.ds(start, GROUP), pl.ds(column, width)],
            dst_ref=owned.at[
                pl.ds(0, early), :, pl.ds(pl.multiple_of(me * blocks + start, GROUP), GROUP), pl.ds(column, width)
            ],
            send_sem=early_send.at[step, k - 1],
            recv_sem=early_recv.at[step, k - 1],
            device_id={"tm": partner(me, k, n_tm)},
            device_id_type=MESH,
        )

    def later_copy(item, k):
        first, size, column, span = later[item]
        columns = pl.ds(column, span)
        return pltpu.make_async_remote_copy(
            src_ref=outgoing.at[k - 1, pl.ds(first, size), :, :, columns],
            dst_ref=owned.at[pl.ds(first, size), :, pl.ds(pl.multiple_of(me * blocks, GROUP), blocks), columns],
            send_sem=unit_send.at[item, k - 1],
            recv_sem=unit_recv.at[item, k - 1],
            device_id={"tm": partner(me, k, n_tm)},
            device_id_type=MESH,
        )

    def sum_copy(unit, k):
        owner = partner(seat, k, n_space)
        return pltpu.make_async_remote_copy(
            src_ref=part.at[unit, owner],
            dst_ref=arrived.at[unit, k - 1],
            send_sem=sum_send.at[unit],
            recv_sem=sum_recv.at[unit],
            device_id={"space": owner},
            device_id_type=MESH,
        )

    constants = [
        pltpu.make_async_copy(pair[0], pair[1], const_sem.at[i])
        for i, pair in enumerate(
            [(table_hbm, table_ref), (w_hbm, w_ref), (swap_hbm, swap_ref), (order_hbm, order_ref)]
        )
    ]
    constants[0].start()
    constants[1].start()
    load(0).start()
    constants[2].start()
    constants[3].start()
    barrier = pltpu.get_barrier_semaphore()
    core = seat + 1 - 2 * lax.rem(seat, 2)
    met = len(peers) + 1 + (seat >= 2).astype(jnp.int32) + (seat + 2 < n_space).astype(jnp.int32)

    def greet(semaphore):
        for k in peers:
            pl.semaphore_signal(semaphore, inc=1, device_id={"tm": partner(me, k, n_tm)}, device_id_type=MESH)
        pl.semaphore_signal(semaphore, inc=1, device_id={"space": core}, device_id_type=MESH)

        @pl.when(seat >= 2)
        def _():
            pl.semaphore_signal(semaphore, inc=1, device_id={"space": seat - 2}, device_id_type=MESH)

        @pl.when(seat + 2 < n_space)
        def _():
            pl.semaphore_signal(semaphore, inc=1, device_id={"space": seat + 2}, device_id_type=MESH)

    greet(barrier)
    for copy in constants:
        copy.wait()

    def transform(step, carry):
        start, column = place(step)

        @pl.when(step + 1 < steps)
        def _():
            load(step + 1).start()

        load(step).wait()
        scale = jnp.sqrt(w_ref[:, pl.ds(column, width)])

        def one(b, inner):
            product = jnp.dot(table_ref[...], x_buf[step % 2, b], preferred_element_type=jnp.float32)
            rows_buf[b] = (product * scale).astype(jnp.bfloat16)
            return inner

        lax.fori_loop(0, GROUP, one, 0, unroll=8)
        def exchange(k, f):
            target = owned if k == 0 else outgoing.at[k - 1]
            base = partner(me, k, n_tm) * freqs
            offset = me * blocks + start if k == 0 else start
            for c in range(2):
                row = pl.multiple_of(c * half + base + f, GROUP)
                taken = rows_buf[:, pl.ds(row, GROUP), :].reshape(GROUP * GROUP, width)
                swapped = jnp.dot(swap_ref[...], taken, preferred_element_type=jnp.float32)
                target[
                    pl.ds(f, GROUP), c, pl.ds(pl.multiple_of(offset, GROUP), GROUP), pl.ds(column, width)
                ] = swapped.astype(jnp.bfloat16).reshape(GROUP, GROUP, width)

        starts = range(0, freqs, GROUP)
        first = [(k, f) for f in starts if f < early for k in peers]
        rest = [(k, f) for f in starts if f >= early for k in peers] + [(0, f) for f in starts]
        for k, f in first:
            exchange(k, f)

        @pl.when(step == 0)
        def _():
            pl.semaphore_wait(barrier, met)
            if rounds > 1:
                greet(round_sem.at[0])

        for k in peers:
            early_copy(step, k).start()
        for k, f in rest:
            exchange(k, f)
        return carry

    lax.fori_loop(0, steps, transform, 0)

    for item in range(len(later)):
        for k in peers:
            later_copy(item, k).start()

    def meet(r, carry):
        pl.semaphore_wait(round_sem.at[r - 1], met)

        @pl.when(r + 1 < rounds)
        def _():
            greet(round_sem.at[r])

        return carry

    lax.fori_loop(1, rounds, meet, 0)

    def early_wait(step, carry):
        for k in range(1, n_tm):
            early_copy(step, k).wait()
        return carry

    lax.fori_loop(0, steps, early_wait, 0)

    def finish(unit):
        pltpu.make_async_copy(arrived.at[unit], arrived.at[unit], sum_recv.at[unit]).wait()
        value = part[unit, seat].astype(jnp.float32)
        for k in range(n_space - 1):
            value = value + arrived[unit, k].astype(jnp.float32)
        for i in range(2 * unit_size):
            out_buf[:, pl.ds(unit * 2 * unit_size + i, 1), :] = value[i * rows : (i + 1) * rows][:, None, :]

    def cross(unit, carry):
        for item in range(len(later) - 1):

            @pl.when(unit == later[item][0] // unit_size)
            def _(item=item):
                for k in peers:
                    later_copy(item, k).wait_recv()

        pieces = []
        grams = []
        for column in (0, points // 2):
            if column:

                @pl.when(unit == units - 1)
                def _():
                    for k in peers:
                        later_copy(len(later) - 1, k).wait_recv()

            for i in range(unit_size):
                both = owned[unit * unit_size + i, :, :, pl.ds(column, points // 2)]
                both = both.reshape(2 * total, points // 2)
                grams.append(
                    lax.dot_general(both, both, (((1,), (1,)), ((), ())), preferred_element_type=jnp.float32)
                )
        for i in range(unit_size):
            gram = grams[i] + grams[unit_size + i]
            pieces.append(gram[:total, :total] + gram[total:, total:])
            pieces.append(gram[:total, total:] - gram[total:, :total])
        pieces = [piece.astype(jnp.bfloat16) for piece in pieces]
        if rows % GROUP == 0:
            for i, piece in enumerate(pieces):
                for d in range(n_space):
                    part[unit, d, i * rows : (i + 1) * rows, :] = piece[d * rows : (d + 1) * rows]
        else:
            ordered = jnp.dot(
                order_ref[...], jnp.concatenate(pieces, axis=0), preferred_element_type=jnp.float32
            )
            part[unit] = ordered.astype(jnp.bfloat16).reshape(n_space, slab, total)

        for k in seats:
            sum_copy(unit, k).start()

        @pl.when(unit > 1)
        def _():
            finish(unit - 2)

        return carry

    lax.fori_loop(0, units, cross, 0)
    for unit in (units - 2, units - 1):
        finish(unit)

    def sent(unit, carry):
        pltpu.make_async_copy(arrived.at[unit], arrived.at[unit], sum_send.at[unit]).wait()
        return carry

    lax.fori_loop(0, units, sent, 0)
    for item in range(len(later)):
        for k in peers:
            later_copy(item, k).wait_send()


def per_device(n_tm, n_space, snapshots, weights):
    blocks, length, points = snapshots.shape
    total, freqs = blocks * n_tm, length // 2 // n_tm
    rows = total // n_space
    unit_size = max(1, GROUP // (2 * rows))
    units = freqs // unit_size
    slab = unit_size * 2 * rows
    width = min(WIDTH, points)
    early = max(freqs // 4, unit_size)
    later, first = [], early
    while first + unit_size < freqs:
        size = max(unit_size, (freqs - first) // (2 * unit_size) * unit_size)
        later.append((first, size, 0, points))
        first += size
    later += [(first, unit_size, column, points // 2) for column in (0, points // 2)]
    steps = blocks // GROUP * (points // width)
    hbm = pl.BlockSpec(memory_space=pl.ANY)
    bf16 = jnp.bfloat16
    table = make_table(length, length // 2)
    swap = swap_matrix()
    order = swap if rows % GROUP == 0 else order_matrix(unit_size, total, n_space)
    sums = pl.pallas_call(
        functools.partial(kernel, n_tm, n_space, width, early, unit_size, later),
        out_shape=pltpu.VMEM((rows, freqs * 2, total), jnp.float32),
        in_specs=[hbm] * 5,
        out_specs=pl.BlockSpec(memory_space=pltpu.VMEM),
        scratch_shapes=[
            pltpu.VMEM((1, points), jnp.float32),
            pltpu.VMEM(table.shape, bf16),
            pltpu.VMEM(swap.shape, bf16),
            pltpu.VMEM(order.shape, bf16),
            pltpu.VMEM((2, GROUP, length, width), bf16),
            pltpu.VMEM((GROUP, length, width), bf16),
            pltpu.VMEM((n_tm - 1, freqs, 2, blocks, points), bf16),
            pltpu.VMEM((freqs, 2, total, points), bf16),
            pltpu.VMEM((units, n_space, slab, total), bf16),
            pltpu.VMEM((units, n_space - 1, slab, total), bf16),
            pltpu.SemaphoreType.DMA((4,)),
            pltpu.SemaphoreType.DMA((2,)),
            pltpu.SemaphoreType.DMA((steps, n_tm - 1)),
            pltpu.SemaphoreType.DMA((steps, n_tm - 1)),
            pltpu.SemaphoreType.DMA((len(later), n_tm - 1)),
            pltpu.SemaphoreType.DMA((len(later), n_tm - 1)),
            pltpu.SemaphoreType.DMA((units,)),
            pltpu.SemaphoreType.DMA((units,)),
            pltpu.SemaphoreType.REGULAR((max(n_space // 2 - 1, 1),)),
        ],
        compiler_params=pltpu.CompilerParams(
            collective_id=0, has_side_effects=True, vmem_limit_bytes=60 * 1024 * 1024
        ),
    )(
        snapshots,
        weights[None, :],
        table,
        swap,
        order,
    )
    return sums.reshape(rows, freqs, 2, total)


def solution(mesh):
    return jax.shard_map(
        functools.partial(per_device, mesh.shape["tm"], mesh.shape["space"]),
        mesh=mesh,
        in_specs=(P("tm", None, "space"), P("space")),
        out_specs=P("space", "tm", None, None),
        check_vma=False,
    )
```

```python
import functools
import math

import jax
import jax.numpy as jnp
import numpy as np
from jax import lax
from jax.experimental import pallas as pl
from jax.experimental.pallas import tpu as pltpu
from jax.sharding import PartitionSpec as P

MESH = pl.DeviceIdType.MESH
WIDTH = 128
GROUP = 16
PART = 8


def make_table(length, count):
    steps_t = np.arange(length, dtype=np.int32)
    freqs = np.arange(count, dtype=np.int32)
    turn = np.float32(2.0 * math.pi / length)
    phase = (freqs[:, None] * steps_t[None, :] % length).astype(np.float32) * turn
    hann = np.float32(0.5) - np.float32(0.5) * np.cos(steps_t.astype(np.float32) * turn)
    factor = np.float32(1.0 / math.sqrt(3.0 * length / 8.0))
    table = np.concatenate([np.cos(phase), -np.sin(phase)], axis=0) * hann[None, :] * factor
    return table.astype(jnp.bfloat16)


def swap_matrix():
    size = GROUP * GROUP
    source = np.arange(size).reshape(GROUP, GROUP).T.reshape(-1)
    return jnp.asarray(np.eye(size, dtype=np.float32)[source].astype(jnp.bfloat16))


def order_matrix(unit_size, blocks, n_space):
    size = unit_size * 2 * blocks
    rows = blocks // n_space
    source = np.arange(size).reshape(unit_size, 2, n_space, rows).transpose(2, 0, 1, 3).reshape(-1)
    return jnp.asarray(np.eye(size, dtype=np.float32)[source].astype(jnp.bfloat16))


def partner(me, k, count):
    if count & (count - 1):
        return lax.rem(me + k, count)
    other, bit = 0, 1
    while bit < count:
        have = lax.rem(lax.div(me, bit), 2)
        other = other + bit * (1 - have if k & bit else have)
        bit *= 2
    return other


def early_batches(blocks, points, width):
    tiles = points // width
    batches = []
    for group in range(blocks // GROUP):
        tile = 0
        while tile < tiles:
            count = tiles if group else max(tile, 1)
            count = min(count, tiles - tile)
            batches.append((group * tiles + tile + count - 1, group * GROUP, tile * width, count * width))
            tile += count
    return batches


def row_order(n_tm, freqs, early):
    peers = range(n_tm - 1, 0, -1)
    starts = range(0, freqs, GROUP)
    first = [(k, f) for f in starts if f < early for k in peers]
    rest = [(k, f) for f in starts if f >= early for k in peers] + [(0, f) for f in starts]
    return first, rest


def ordered_tables(table, n_tm, freqs, early):
    first, rest = row_order(n_tm, freqs, early)
    tables = []
    for me in range(n_tm):
        owners = [((me + k) % n_tm if n_tm & (n_tm - 1) else me ^ k, f) for k, f in first + rest]
        rows = [c * n_tm * freqs + owner * freqs + f + np.arange(GROUP) for owner, f in owners for c in range(2)]
        tables.append(table[np.concatenate(rows)])
    return jnp.asarray(np.stack(tables))


def kernel(
    n_tm, n_space, width, early, unit_size, batches, later,
    x_ref, w_hbm, table_hbm, swap_hbm, order_hbm, out_buf,
    w_ref, table_ref, swap_ref, order_ref,
    x_buf, rows_buf, outgoing, owned, part, arrived,
    const_sem, x_sem, early_send, early_recv, unit_send, unit_recv, sum_send, sum_recv, round_sem,
):
    me = lax.axis_index("tm")
    seat = lax.axis_index("space")
    blocks, length, points = x_ref.shape
    half = length // 2
    freqs = half // n_tm
    tiles = points // width
    steps = blocks // GROUP * tiles
    units = freqs // unit_size
    total = blocks * n_tm
    rows = total // n_space
    slab = unit_size * 2 * rows
    peers = list(range(n_tm - 1, 0, -1))
    rounds = n_space // 2
    seats = list(range(n_space - 1, 0, -1))

    def place(step):
        start = pl.multiple_of(step // tiles * GROUP, GROUP)
        return start, pl.multiple_of(step % tiles * width, width)

    def load(step, part):
        start, column = place(step)
        return pltpu.make_async_copy(
            x_ref.at[pl.ds(start + part * PART, PART), :, pl.ds(column, width)],
            x_buf.at[step % 2, pl.ds(part * PART, PART)],
            x_sem.at[step % 2, part],
        )

    def early_copy(item, k):
        _, start, column, span = batches[item]
        columns = pl.ds(column, span)
        return pltpu.make_async_remote_copy(
            src_ref=outgoing.at[k - 1, pl.ds(0, early), :, pl.ds(start, GROUP), columns],
            dst_ref=owned.at[
                pl.ds(0, early), :, pl.ds(pl.multiple_of(me * blocks + start, GROUP), GROUP), columns
            ],
            send_sem=early_send.at[item, k - 1],
            recv_sem=early_recv.at[item, k - 1],
            device_id={"tm": partner(me, k, n_tm)},
            device_id_type=MESH,
        )

    def later_copy(item, k):
        first, size, column, span = later[item]
        columns = pl.ds(column, span)
        return pltpu.make_async_remote_copy(
            src_ref=outgoing.at[k - 1, pl.ds(first, size), :, :, columns],
            dst_ref=owned.at[pl.ds(first, size), :, pl.ds(pl.multiple_of(me * blocks, GROUP), blocks), columns],
            send_sem=unit_send.at[item, k - 1],
            recv_sem=unit_recv.at[item, k - 1],
            device_id={"tm": partner(me, k, n_tm)},
            device_id_type=MESH,
        )

    def sum_copy(unit, k):
        owner = partner(seat, k, n_space)
        return pltpu.make_async_remote_copy(
            src_ref=part.at[unit, owner],
            dst_ref=arrived.at[unit, k - 1],
            send_sem=sum_send.at[unit],
            recv_sem=sum_recv.at[unit],
            device_id={"space": owner},
            device_id_type=MESH,
        )

    first, rest = row_order(n_tm, freqs, early)
    place_of = {pair: i for i, pair in enumerate(first + rest)}
    split = len(first) * 2 * GROUP
    constants = [
        pltpu.make_async_copy(pair[0], pair[1], const_sem.at[i])
        for i, pair in enumerate(
            [(table_hbm.at[me], table_ref), (w_hbm, w_ref), (swap_hbm, swap_ref), (order_hbm, order_ref)]
        )
    ]
    load(0, 0).start()
    constants[0].start()
    constants[1].start()
    for q in range(1, GROUP // PART):
        load(0, q).start()
    constants[2].start()
    constants[3].start()
    barrier = pltpu.get_barrier_semaphore()
    core = seat + 1 - 2 * lax.rem(seat, 2)
    met = len(peers) + 1 + (seat >= 2).astype(jnp.int32) + (seat + 2 < n_space).astype(jnp.int32)

    def greet(semaphore):
        for k in peers:
            pl.semaphore_signal(semaphore, inc=1, device_id={"tm": partner(me, k, n_tm)}, device_id_type=MESH)
        pl.semaphore_signal(semaphore, inc=1, device_id={"space": core}, device_id_type=MESH)

        @pl.when(seat >= 2)
        def _():
            pl.semaphore_signal(semaphore, inc=1, device_id={"space": seat - 2}, device_id_type=MESH)

        @pl.when(seat + 2 < n_space)
        def _():
            pl.semaphore_signal(semaphore, inc=1, device_id={"space": seat + 2}, device_id_type=MESH)

    greet(barrier)
    for copy in constants[:2]:
        copy.wait()

    def transform(step, carry):
        start, column = place(step)

        @pl.when(step + 1 < steps)
        def _():
            for q in range(GROUP // PART):
                load(step + 1, q).start()

        scale = jnp.sqrt(w_ref[:, pl.ds(column, width)])

        def product(b, low, high):
            value = jnp.dot(table_ref[low:high], x_buf[step % 2, b], preferred_element_type=jnp.float32)
            rows_buf[b, low:high] = (value * scale).astype(jnp.bfloat16)

        def exchange(k, f):
            target = owned if k == 0 else outgoing.at[k - 1]
            offset = me * blocks + start if k == 0 else start
            for c in range(2):
                row = (2 * place_of[k, f] + c) * GROUP
                taken = rows_buf[:, row : row + GROUP, :].reshape(GROUP * GROUP, width)
                swapped = jnp.dot(swap_ref[...], taken, preferred_element_type=jnp.float32)
                target[
                    pl.ds(f, GROUP), c, pl.ds(pl.multiple_of(offset, GROUP), GROUP), pl.ds(column, width)
                ] = swapped.astype(jnp.bfloat16).reshape(GROUP, GROUP, width)

        for q in range(GROUP // PART):
            load(step, q).wait()
            for b in range(q * PART, (q + 1) * PART):
                product(b, 0, split)
        @pl.when(step == 0)
        def _():
            for copy in constants[2:]:
                copy.wait()

        for k, f in first:
            exchange(k, f)

        @pl.when(step == 0)
        def _():
            pl.semaphore_wait(barrier, met)
            if rounds > 1:
                greet(round_sem.at[0])

        for item in range(len(batches)):

            @pl.when(step == batches[item][0])
            def _(item=item):
                for k in peers:
                    early_copy(item, k).start()

        def second(b, inner):
            product(b, split, length)
            return inner

        lax.fori_loop(0, GROUP, second, 0, unroll=16)
        for k, f in rest:
            exchange(k, f)
        return carry

    lax.fori_loop(0, steps, transform, 0)

    for item in range(len(later)):
        for k in peers:
            later_copy(item, k).start()

    def meet(r, carry):
        pl.semaphore_wait(round_sem.at[r - 1], met)

        @pl.when(r + 1 < rounds)
        def _():
            greet(round_sem.at[r])

        return carry

    lax.fori_loop(1, rounds, meet, 0)

    for item in range(len(batches)):
        for k in peers:
            early_copy(item, k).wait()

    def finish(unit):
        pltpu.make_async_copy(arrived.at[unit], arrived.at[unit], sum_recv.at[unit]).wait()
        value = part[unit, seat].astype(jnp.float32)
        for k in range(n_space - 1):
            value = value + arrived[unit, k].astype(jnp.float32)
        for i in range(2 * unit_size):
            out_buf[:, pl.ds(unit * 2 * unit_size + i, 1), :] = value[i * rows : (i + 1) * rows][:, None, :]

    def cross(unit, carry):
        for item in range(len(later) - 1):

            @pl.when(unit == later[item][0] // unit_size)
            def _(item=item):
                for k in peers:
                    later_copy(item, k).wait_recv()

        pieces = []
        grams = []
        for column in (0, points // 2):
            if column:

                @pl.when(unit == units - 1)
                def _():
                    for k in peers:
                        later_copy(len(later) - 1, k).wait_recv()

            for i in range(unit_size):
                both = owned[unit * unit_size + i, :, :, pl.ds(column, points // 2)]
                both = both.reshape(2 * total, points // 2)
                grams.append(
                    lax.dot_general(both, both, (((1,), (1,)), ((), ())), preferred_element_type=jnp.float32)
                )
        for i in range(unit_size):
            gram = grams[i] + grams[unit_size + i]
            pieces.append(gram[:total, :total] + gram[total:, total:])
            pieces.append(gram[:total, total:] - gram[total:, :total])
        pieces = [piece.astype(jnp.bfloat16) for piece in pieces]
        if rows % GROUP == 0:
            for i, piece in enumerate(pieces):
                for d in range(n_space):
                    part[unit, d, i * rows : (i + 1) * rows, :] = piece[d * rows : (d + 1) * rows]
        else:
            ordered = jnp.dot(
                order_ref[...], jnp.concatenate(pieces, axis=0), preferred_element_type=jnp.float32
            )
            part[unit] = ordered.astype(jnp.bfloat16).reshape(n_space, slab, total)

        for k in seats:
            sum_copy(unit, k).start()

        @pl.when(unit > 1)
        def _():
            finish(unit - 2)

        return carry

    lax.fori_loop(0, units, cross, 0)
    for unit in (units - 2, units - 1):
        finish(unit)

    def sent(unit, carry):
        pltpu.make_async_copy(arrived.at[unit], arrived.at[unit], sum_send.at[unit]).wait()
        return carry

    lax.fori_loop(0, units, sent, 0)
    for item in range(len(later)):
        for k in peers:
            later_copy(item, k).wait_send()


def per_device(n_tm, n_space, snapshots, weights):
    blocks, length, points = snapshots.shape
    total, freqs = blocks * n_tm, length // 2 // n_tm
    rows = total // n_space
    unit_size = max(1, GROUP // (2 * rows))
    units = freqs // unit_size
    slab = unit_size * 2 * rows
    width = min(WIDTH, points)
    early = max(freqs // 2, unit_size)
    later, first = [], early
    while first + unit_size < freqs:
        size = max(unit_size, (freqs - first) // (2 * unit_size) * unit_size)
        later.append((first, size, 0, points))
        first += size
    later += [(first, unit_size, column, points // 2) for column in (0, points // 2)]
    batches = early_batches(blocks, points, width)
    hbm = pl.BlockSpec(memory_space=pl.ANY)
    bf16 = jnp.bfloat16
    table = ordered_tables(make_table(length, length // 2), n_tm, freqs, early)
    swap = swap_matrix()
    order = swap if rows % GROUP == 0 else order_matrix(unit_size, total, n_space)
    sums = pl.pallas_call(
        functools.partial(kernel, n_tm, n_space, width, early, unit_size, batches, later),
        out_shape=pltpu.VMEM((rows, freqs * 2, total), jnp.float32),
        in_specs=[hbm] * 5,
        out_specs=pl.BlockSpec(memory_space=pltpu.VMEM),
        scratch_shapes=[
            pltpu.VMEM((1, points), jnp.float32),
            pltpu.VMEM(table.shape[1:], bf16),
            pltpu.VMEM(swap.shape, bf16),
            pltpu.VMEM(order.shape, bf16),
            pltpu.VMEM((2, GROUP, length, width), bf16),
            pltpu.VMEM((GROUP, length, width), bf16),
            pltpu.VMEM((n_tm - 1, freqs, 2, blocks, points), bf16),
            pltpu.VMEM((freqs, 2, total, points), bf16),
            pltpu.VMEM((units, n_space, slab, total), bf16),
            pltpu.VMEM((units, n_space - 1, slab, total), bf16),
            pltpu.SemaphoreType.DMA((4,)),
            pltpu.SemaphoreType.DMA((2, GROUP // PART)),
            pltpu.SemaphoreType.DMA((len(batches), n_tm - 1)),
            pltpu.SemaphoreType.DMA((len(batches), n_tm - 1)),
            pltpu.SemaphoreType.DMA((len(later), n_tm - 1)),
            pltpu.SemaphoreType.DMA((len(later), n_tm - 1)),
            pltpu.SemaphoreType.DMA((units,)),
            pltpu.SemaphoreType.DMA((units,)),
            pltpu.SemaphoreType.REGULAR((max(n_space // 2 - 1, 1),)),
        ],
        compiler_params=pltpu.CompilerParams(
            collective_id=0, has_side_effects=True, vmem_limit_bytes=60 * 1024 * 1024
        ),
    )(
        snapshots,
        weights[None, :],
        table,
        swap,
        order,
    )
    return sums.reshape(rows, freqs, 2, total)


def solution(mesh):
    return jax.shard_map(
        functools.partial(per_device, mesh.shape["tm"], mesh.shape["space"]),
        mesh=mesh,
        in_specs=(P("tm", None, "space"), P("space")),
        out_specs=P("space", "tm", None, None),
        check_vma=False,
    )
```

```python
import functools
import math

import jax
import jax.numpy as jnp
import numpy as np
from jax import lax
from jax.experimental import pallas as pl
from jax.experimental.pallas import tpu as pltpu
from jax.sharding import PartitionSpec as P

MESH = pl.DeviceIdType.MESH
WIDTH = 128
GROUP = 16
PART = 8
SHARES = 2


def make_table(length, count):
    steps_t = np.arange(length, dtype=np.int32)
    freqs = np.arange(count, dtype=np.int32)
    turn = np.float32(2.0 * math.pi / length)
    phase = (freqs[:, None] * steps_t[None, :] % length).astype(np.float32) * turn
    hann = np.float32(0.5) - np.float32(0.5) * np.cos(steps_t.astype(np.float32) * turn)
    factor = np.float32(1.0 / math.sqrt(3.0 * length / 8.0))
    table = np.concatenate([np.cos(phase), -np.sin(phase)], axis=0) * hann[None, :] * factor
    return table.astype(jnp.bfloat16)


def swap_matrix():
    size = GROUP * GROUP
    source = np.arange(size).reshape(GROUP, GROUP).T.reshape(-1)
    return jnp.asarray(np.eye(size, dtype=np.float32)[source].astype(jnp.bfloat16))


def order_matrix(unit_size, blocks, n_space):
    size = unit_size * 2 * blocks
    rows = blocks // n_space
    source = np.arange(size).reshape(unit_size, 2, n_space, rows).transpose(2, 0, 1, 3).reshape(-1)
    return jnp.asarray(np.eye(size, dtype=np.float32)[source].astype(jnp.bfloat16))


def partner(me, k, count):
    if count & (count - 1):
        return lax.rem(me + k, count)
    other, bit = 0, 1
    while bit < count:
        have = lax.rem(lax.div(me, bit), 2)
        other = other + bit * (1 - have if k & bit else have)
        bit *= 2
    return other


def early_batches(blocks, points, width):
    tiles = points // width
    batches = []
    for group in range(blocks // GROUP):
        tile = 0
        while tile < tiles:
            count = tiles if group else max(tile, 1)
            count = min(count, tiles - tile)
            batches.append((group * tiles + tile + count - 1, group * GROUP, tile * width, count * width))
            tile += count
    return batches


def moving(n_space):
    return n_space >= 8


def row_order(n_tm, freqs, early):
    peers = range(n_tm - 1, 0, -1)
    starts = range(0, freqs, GROUP)
    first = [(k, f) for f in starts if f < early for k in peers]
    rest = [(k, f) for f in starts if f >= early for k in peers] + [(0, f) for f in starts]
    return first, rest


def ordered_tables(table, n_tm, freqs, early):
    first, rest = row_order(n_tm, freqs, early)
    tables = []
    for me in range(n_tm):
        owners = [((me + k) % n_tm if n_tm & (n_tm - 1) else me ^ k, f) for k, f in first + rest]
        rows = [c * n_tm * freqs + owner * freqs + f + np.arange(GROUP) for owner, f in owners for c in range(2)]
        tables.append(table[np.concatenate(rows)])
    return jnp.asarray(np.stack(tables))


def kernel(
    n_tm, n_space, width, early, unit_size, batches, later,
    x_ref, w_hbm, table_hbm, swap_hbm, order_hbm, out_buf,
    w_ref, table_ref, swap_ref, order_ref,
    x_buf, rows_buf, outgoing, owned, part, arrived, spare_out, spare,
    const_sem, x_sem, early_send, early_recv, unit_send, unit_recv, sum_send, sum_recv, round_sem,
    move_send, move_recv, spare_send, spare_recv,
):
    me = lax.axis_index("tm")
    seat = lax.axis_index("space")
    blocks, length, points = x_ref.shape
    half = length // 2
    freqs = half // n_tm
    tiles = points // width
    steps = blocks // GROUP * tiles
    units = freqs // unit_size
    total = blocks * n_tm
    rows = total // n_space
    slab = unit_size * 2 * rows
    peers = list(range(n_tm - 1, 0, -1))
    rounds = n_space // 2
    moved = SHARES * spare.shape[-1]
    cut = points - moved
    last_first = freqs - unit_size
    share = moved // SHARES
    gives = [seat >= n_space - 2, seat >= n_space - 4]
    takes = [seat < 2, seat < 4]
    taker = jnp.where(gives[0], seat - (n_space - 2), seat - (n_space - 6))
    seats = list(range(n_space - 1, 0, -1))

    def place(step):
        start = pl.multiple_of(step // tiles * GROUP, GROUP)
        return start, pl.multiple_of(step % tiles * width, width)

    def load(step, part):
        start, column = place(step)
        return pltpu.make_async_copy(
            x_ref.at[pl.ds(start + part * PART, PART), :, pl.ds(column, width)],
            x_buf.at[step % 2, pl.ds(part * PART, PART)],
            x_sem.at[step % 2, part],
        )

    def early_copy(item, k):
        _, start, column, span = batches[item]
        columns = pl.ds(column, span)
        return pltpu.make_async_remote_copy(
            src_ref=outgoing.at[k - 1, pl.ds(0, early), :, pl.ds(start, GROUP), columns],
            dst_ref=owned.at[
                pl.ds(0, early), :, pl.ds(pl.multiple_of(me * blocks + start, GROUP), GROUP), columns
            ],
            send_sem=early_send.at[item, k - 1],
            recv_sem=early_recv.at[item, k - 1],
            device_id={"tm": partner(me, k, n_tm)},
            device_id_type=MESH,
        )

    def later_copy(item, k):
        first, size, column, span = later[item]
        columns = pl.ds(column, span)
        return pltpu.make_async_remote_copy(
            src_ref=outgoing.at[k - 1, pl.ds(first, size), :, :, columns],
            dst_ref=owned.at[pl.ds(first, size), :, pl.ds(pl.multiple_of(me * blocks, GROUP), blocks), columns],
            send_sem=unit_send.at[item, k - 1],
            recv_sem=unit_recv.at[item, k - 1],
            device_id={"tm": partner(me, k, n_tm)},
            device_id_type=MESH,
        )

    def move_copy(i, k):
        columns = pl.ds(cut + i * share, share)
        mine = pl.ds(pl.multiple_of(me * blocks, GROUP), blocks)
        if k:
            source = outgoing.at[k - 1, pl.ds(last_first, unit_size), :, :, columns]
            target = spare_out.at[i, k - 1]
        else:
            source = owned.at[pl.ds(last_first, unit_size), :, mine, columns]
            target = spare.at[i, :, :, mine]
        return pltpu.make_async_remote_copy(
            src_ref=source,
            dst_ref=target,
            send_sem=move_send.at[i, k],
            recv_sem=move_recv.at[i, k],
            device_id={"space": taker},
            device_id_type=MESH,
        )

    def spare_copy(i, k):
        return pltpu.make_async_remote_copy(
            src_ref=spare_out.at[i, k - 1],
            dst_ref=spare.at[i, :, :, pl.ds(pl.multiple_of(me * blocks, GROUP), blocks)],
            send_sem=spare_send.at[i, k - 1],
            recv_sem=spare_recv.at[i, k - 1],
            device_id={"tm": partner(me, k, n_tm)},
            device_id_type=MESH,
        )

    def sum_copy(unit, k):
        owner = partner(seat, k, n_space)
        return pltpu.make_async_remote_copy(
            src_ref=part.at[unit, owner],
            dst_ref=arrived.at[unit, k - 1],
            send_sem=sum_send.at[unit],
            recv_sem=sum_recv.at[unit],
            device_id={"space": owner},
            device_id_type=MESH,
        )

    first, rest = row_order(n_tm, freqs, early)
    place_of = {pair: i for i, pair in enumerate(first + rest)}
    split = len(first) * 2 * GROUP
    constants = [
        pltpu.make_async_copy(pair[0], pair[1], const_sem.at[i])
        for i, pair in enumerate(
            [(table_hbm.at[me], table_ref), (w_hbm, w_ref), (swap_hbm, swap_ref), (order_hbm, order_ref)]
        )
    ]
    load(0, 0).start()
    constants[0].start()
    constants[1].start()
    for q in range(1, GROUP // PART):
        load(0, q).start()
    constants[2].start()
    constants[3].start()
    barrier = pltpu.get_barrier_semaphore()
    core = seat + 1 - 2 * lax.rem(seat, 2)
    met = len(peers) + 1 + (seat >= 2).astype(jnp.int32) + (seat + 2 < n_space).astype(jnp.int32)

    def greet(semaphore):
        for k in peers:
            pl.semaphore_signal(semaphore, inc=1, device_id={"tm": partner(me, k, n_tm)}, device_id_type=MESH)
        pl.semaphore_signal(semaphore, inc=1, device_id={"space": core}, device_id_type=MESH)

        @pl.when(seat >= 2)
        def _():
            pl.semaphore_signal(semaphore, inc=1, device_id={"space": seat - 2}, device_id_type=MESH)

        @pl.when(seat + 2 < n_space)
        def _():
            pl.semaphore_signal(semaphore, inc=1, device_id={"space": seat + 2}, device_id_type=MESH)

    greet(barrier)
    for copy in constants[:2]:
        copy.wait()

    def transform(step, carry):
        start, column = place(step)

        @pl.when(step + 1 < steps)
        def _():
            for q in range(GROUP // PART):
                load(step + 1, q).start()

        scale = jnp.sqrt(w_ref[:, pl.ds(column, width)])

        def product(b, low, high):
            value = jnp.dot(table_ref[low:high], x_buf[step % 2, b], preferred_element_type=jnp.float32)
            rows_buf[b, low:high] = (value * scale).astype(jnp.bfloat16)

        def exchange(k, f):
            target = owned if k == 0 else outgoing.at[k - 1]
            offset = me * blocks + start if k == 0 else start
            for c in range(2):
                row = (2 * place_of[k, f] + c) * GROUP
                taken = rows_buf[:, row : row + GROUP, :].reshape(GROUP * GROUP, width)
                swapped = jnp.dot(swap_ref[...], taken, preferred_element_type=jnp.float32)
                target[
                    pl.ds(f, GROUP), c, pl.ds(pl.multiple_of(offset, GROUP), GROUP), pl.ds(column, width)
                ] = swapped.astype(jnp.bfloat16).reshape(GROUP, GROUP, width)

        for q in range(GROUP // PART):
            load(step, q).wait()
            for b in range(q * PART, (q + 1) * PART):
                product(b, 0, split)
        @pl.when(step == 0)
        def _():
            for copy in constants[2:]:
                copy.wait()

        for k, f in first:
            exchange(k, f)

        @pl.when(step == 0)
        def _():
            pl.semaphore_wait(barrier, met)
            if rounds > 1:
                greet(round_sem.at[0])

        for item in range(len(batches)):

            @pl.when(step == batches[item][0])
            def _(item=item):
                for k in peers:
                    early_copy(item, k).start()

        def second(b, inner):
            product(b, split, length)
            return inner

        lax.fori_loop(0, GROUP, second, 0, unroll=16)
        for k, f in rest:
            exchange(k, f)
        return carry

    lax.fori_loop(0, steps, transform, 0)

    def meet(r, carry):
        pl.semaphore_wait(round_sem.at[r - 1], met)

        @pl.when(r + 1 < rounds)
        def _():
            greet(round_sem.at[r])

        return carry

    lax.fori_loop(1, rounds, meet, 0)

    if moving(n_space):
        for i in range(SHARES):

            @pl.when(gives[i])
            def _(i=i):
                for k in range(n_tm):
                    move_copy(i, k).start()

        for i in range(SHARES):

            @pl.when(takes[i])
            def _(i=i):
                for k in range(n_tm):
                    move_copy(i, k).wait_recv()
                for k in peers:
                    spare_copy(i, k).start()

            @pl.when(jnp.logical_not(takes[i]))
            def _(i=i):
                spare[i] = jnp.zeros(spare.shape[1:], jnp.bfloat16)

            @pl.when(gives[i])
            def _(i=i):
                for k in range(n_tm):
                    move_copy(i, k).wait_send()
                owned[last_first:, :, :, cut + i * share : cut + (i + 1) * share] = jnp.zeros(
                    (unit_size, 2, total, share), jnp.bfloat16
                )

    def own_shares(act):
        for i in range(SHARES):

            @pl.when(jnp.logical_not(gives[i]) if moving(n_space) else True)
            def _(i=i):
                for k in peers:
                    act(later_copy(len(later) - SHARES + i, k))

    def spare_shares(act):
        if moving(n_space):
            for i in range(SHARES):

                @pl.when(takes[i])
                def _(i=i):
                    for k in peers:
                        act(spare_copy(i, k))

    for item in range(len(later) - SHARES):
        for k in peers:
            later_copy(item, k).start()
    own_shares(lambda copy: copy.start())

    for item in range(len(batches)):
        for k in peers:
            early_copy(item, k).wait()

    def finish(unit):
        pltpu.make_async_copy(arrived.at[unit], arrived.at[unit], sum_recv.at[unit]).wait()
        value = part[unit, seat].astype(jnp.float32)
        for k in range(n_space - 1):
            value = value + arrived[unit, k].astype(jnp.float32)
        for i in range(2 * unit_size):
            out_buf[:, pl.ds(unit * 2 * unit_size + i, 1), :] = value[i * rows : (i + 1) * rows][:, None, :]

    def cross(unit, last):
        for item in range(len(later) - SHARES):
            if last:
                if item == len(later) - SHARES - 1:
                    for k in peers:
                        later_copy(item, k).wait_recv()
            elif item < len(later) - SHARES - 1:

                @pl.when(unit == later[item][0] // unit_size)
                def _(item=item):
                    for k in peers:
                        later_copy(item, k).wait_recv()

        pieces = []
        grams = []
        middle = cut if last else points // 2
        for low, high in ((0, middle), (middle, points)):
            if low and last:
                spare_shares(lambda copy: copy.wait_recv())
                own_shares(lambda copy: copy.wait_recv())
            for i in range(unit_size):
                both = owned[unit * unit_size + i, :, :, pl.ds(low, high - low)].reshape(2 * total, high - low)
                if low and last and moving(n_space):
                    extra = [spare[j, i].reshape(2 * total, share) for j in range(SHARES)]
                    both = jnp.concatenate([both] + extra, axis=1)
                grams.append(
                    lax.dot_general(both, both, (((1,), (1,)), ((), ())), preferred_element_type=jnp.float32)
                )
        for i in range(unit_size):
            gram = grams[i] + grams[unit_size + i]
            pieces.append(gram[:total, :total] + gram[total:, total:])
            pieces.append(gram[:total, total:] - gram[total:, :total])
        pieces = [piece.astype(jnp.bfloat16) for piece in pieces]
        if rows % GROUP == 0:
            for i, piece in enumerate(pieces):
                for d in range(n_space):
                    part[unit, d, i * rows : (i + 1) * rows, :] = piece[d * rows : (d + 1) * rows]
        else:
            ordered = jnp.dot(
                order_ref[...], jnp.concatenate(pieces, axis=0), preferred_element_type=jnp.float32
            )
            part[unit] = ordered.astype(jnp.bfloat16).reshape(n_space, slab, total)

        for k in seats:
            sum_copy(unit, k).start()

        if last:
            finish(unit - 2)
        else:

            @pl.when(unit > 1)
            def _():
                finish(unit - 2)

    def cross_step(unit, carry):
        cross(unit, False)
        return carry

    lax.fori_loop(0, units - 1, cross_step, 0)
    cross(units - 1, True)
    for unit in (units - 2, units - 1):
        finish(unit)

    def sent(unit, carry):
        pltpu.make_async_copy(arrived.at[unit], arrived.at[unit], sum_send.at[unit]).wait()
        return carry

    lax.fori_loop(0, units, sent, 0)
    for item in range(len(later) - SHARES):
        for k in peers:
            later_copy(item, k).wait_send()
    spare_shares(lambda copy: copy.wait_send())
    own_shares(lambda copy: copy.wait_send())


def per_device(n_tm, n_space, snapshots, weights):
    blocks, length, points = snapshots.shape
    total, freqs = blocks * n_tm, length // 2 // n_tm
    rows = total // n_space
    unit_size = max(1, GROUP // (2 * rows))
    units = freqs // unit_size
    slab = unit_size * 2 * rows
    width = min(WIDTH, points)
    early = max(freqs // 2, unit_size)
    later, first = [], early
    while first + unit_size < freqs:
        size = max(unit_size, (freqs - first) // (2 * unit_size) * unit_size)
        later.append((first, size, 0, points))
        first += size
    moved = points // 4
    share = moved // SHARES
    later.append((first, unit_size, 0, points - moved))
    later += [(first, unit_size, points - moved + i * share, share) for i in range(SHARES)]
    batches = early_batches(blocks, points, width)
    hbm = pl.BlockSpec(memory_space=pl.ANY)
    bf16 = jnp.bfloat16
    table = ordered_tables(make_table(length, length // 2), n_tm, freqs, early)
    swap = swap_matrix()
    order = swap if rows % GROUP == 0 else order_matrix(unit_size, total, n_space)
    sums = pl.pallas_call(
        functools.partial(kernel, n_tm, n_space, width, early, unit_size, batches, later),
        out_shape=pltpu.VMEM((rows, freqs * 2, total), jnp.float32),
        in_specs=[hbm] * 5,
        out_specs=pl.BlockSpec(memory_space=pltpu.VMEM),
        scratch_shapes=[
            pltpu.VMEM((1, points), jnp.float32),
            pltpu.VMEM(table.shape[1:], bf16),
            pltpu.VMEM(swap.shape, bf16),
            pltpu.VMEM(order.shape, bf16),
            pltpu.VMEM((2, GROUP, length, width), bf16),
            pltpu.VMEM((GROUP, length, width), bf16),
            pltpu.VMEM((n_tm - 1, freqs, 2, blocks, points), bf16),
            pltpu.VMEM((freqs, 2, total, points), bf16),
            pltpu.VMEM((units, n_space, slab, total), bf16),
            pltpu.VMEM((units, n_space - 1, slab, total), bf16),
            pltpu.VMEM((SHARES, n_tm - 1, unit_size, 2, blocks, share), bf16),
            pltpu.VMEM((SHARES, unit_size, 2, total, share), bf16),
            pltpu.SemaphoreType.DMA((4,)),
            pltpu.SemaphoreType.DMA((2, GROUP // PART)),
            pltpu.SemaphoreType.DMA((len(batches), n_tm - 1)),
            pltpu.SemaphoreType.DMA((len(batches), n_tm - 1)),
            pltpu.SemaphoreType.DMA((len(later), n_tm - 1)),
            pltpu.SemaphoreType.DMA((len(later), n_tm - 1)),
            pltpu.SemaphoreType.DMA((units,)),
            pltpu.SemaphoreType.DMA((units,)),
            pltpu.SemaphoreType.REGULAR((max(n_space // 2 - 1, 1),)),
            pltpu.SemaphoreType.DMA((SHARES, n_tm)),
            pltpu.SemaphoreType.DMA((SHARES, n_tm)),
            pltpu.SemaphoreType.DMA((SHARES, n_tm - 1)),
            pltpu.SemaphoreType.DMA((SHARES, n_tm - 1)),
        ],
        compiler_params=pltpu.CompilerParams(
            collective_id=0, has_side_effects=True, vmem_limit_bytes=60 * 1024 * 1024
        ),
    )(
        snapshots,
        weights[None, :],
        table,
        swap,
        order,
    )
    return sums.reshape(rows, freqs, 2, total)


def solution(mesh):
    return jax.shard_map(
        functools.partial(per_device, mesh.shape["tm"], mesh.shape["space"]),
        mesh=mesh,
        in_specs=(P("tm", None, "space"), P("space")),
        out_specs=P("space", "tm", None, None),
        check_vma=False,
    )
```

```python
import functools
import math

import jax
import jax.numpy as jnp
import numpy as np
from jax import lax
from jax.experimental import pallas as pl
from jax.experimental.pallas import tpu as pltpu
from jax.sharding import PartitionSpec as P

MESH = pl.DeviceIdType.MESH
WIDTH = 128
GROUP = 16
PART = 8
SHARES = 2


def make_table(length, count):
    steps_t = np.arange(length, dtype=np.int32)
    freqs = np.arange(count, dtype=np.int32)
    turn = np.float32(2.0 * math.pi / length)
    phase = (freqs[:, None] * steps_t[None, :] % length).astype(np.float32) * turn
    hann = np.float32(0.5) - np.float32(0.5) * np.cos(steps_t.astype(np.float32) * turn)
    factor = np.float32(1.0 / math.sqrt(3.0 * length / 8.0))
    table = np.concatenate([np.cos(phase), -np.sin(phase)], axis=0) * hann[None, :] * factor
    return table.astype(jnp.bfloat16)


def swap_matrix():
    size = GROUP * GROUP
    source = np.arange(size).reshape(GROUP, GROUP).T.reshape(-1)
    return jnp.asarray(np.eye(size, dtype=np.float32)[source].astype(jnp.bfloat16))


def order_matrix(unit_size, blocks, n_space):
    size = unit_size * 2 * blocks
    rows = blocks // n_space
    source = np.arange(size).reshape(unit_size, 2, n_space, rows).transpose(2, 0, 1, 3).reshape(-1)
    return jnp.asarray(np.eye(size, dtype=np.float32)[source].astype(jnp.bfloat16))


def partner(me, k, count):
    if count & (count - 1):
        return lax.rem(me + k, count)
    other, bit = 0, 1
    while bit < count:
        have = lax.rem(lax.div(me, bit), 2)
        other = other + bit * (1 - have if k & bit else have)
        bit *= 2
    return other


def early_batches(blocks, points, width):
    tiles = points // width
    batches = []
    for group in range(blocks // GROUP):
        tile = 0
        while tile < tiles:
            count = tiles if group else max(tile, 1)
            count = min(count, tiles - tile)
            batches.append((group * tiles + tile + count - 1, group * GROUP, tile * width, count * width))
            tile += count
    return batches


def moving(n_space):
    return n_space >= 8


def row_order(n_tm, freqs, early):
    peers = range(n_tm - 1, 0, -1)
    starts = range(0, freqs, GROUP)
    first = [(k, f) for f in starts if f < early for k in peers]
    rest = [(k, f) for f in starts if f >= early for k in peers] + [(0, f) for f in starts]
    return first, rest


def ordered_tables(table, n_tm, freqs, early):
    first, rest = row_order(n_tm, freqs, early)
    tables = []
    for me in range(n_tm):
        owners = [((me + k) % n_tm if n_tm & (n_tm - 1) else me ^ k, f) for k, f in first + rest]
        rows = [c * n_tm * freqs + owner * freqs + f + np.arange(GROUP) for owner, f in owners for c in range(2)]
        tables.append(table[np.concatenate(rows)])
    return jnp.asarray(np.stack(tables))


def kernel(
    n_tm, n_space, width, early, unit_size, batches, later, groups,
    x_ref, w_hbm, table_hbm, swap_hbm, order_hbm, out_buf,
    w_ref, table_ref, swap_ref, order_ref,
    x_buf, rows_buf, outgoing, owned, part, arrived, spare_out, spare,
    const_sem, x_sem, early_sem, unit_send, unit_recv, sum_send, sum_recv, round_sem,
    move_send, move_recv, spare_send, spare_recv,
):
    me = lax.axis_index("tm")
    seat = lax.axis_index("space")
    blocks, length, points = x_ref.shape
    half = length // 2
    freqs = half // n_tm
    tiles = points // width
    steps = blocks // GROUP * tiles
    units = freqs // unit_size
    total = blocks * n_tm
    rows = total // n_space
    slab = unit_size * 2 * rows
    peers = list(range(n_tm - 1, 0, -1))
    rounds = n_space // 2
    moved = SHARES * spare.shape[-1]
    cut = points - moved
    last_first = freqs - unit_size
    share = moved // SHARES
    gives = [seat >= n_space - 2, seat >= n_space - 4]
    takes = [seat < 2, seat < 4]
    taker = jnp.where(gives[0], seat - (n_space - 2), seat - (n_space - 6))
    seats = list(range(n_space - 1, 0, -1))

    def place(step):
        start = pl.multiple_of(step // tiles * GROUP, GROUP)
        return start, pl.multiple_of(step % tiles * width, width)

    def load(step, part):
        start, column = place(step)
        return pltpu.make_async_copy(
            x_ref.at[pl.ds(start + part * PART, PART), :, pl.ds(column, width)],
            x_buf.at[step % 2, pl.ds(part * PART, PART)],
            x_sem.at[step % 2, part],
        )

    def early_copy(item, k):
        _, start, column, span = batches[item]
        columns = pl.ds(column, span)
        return pltpu.make_async_remote_copy(
            src_ref=outgoing.at[k - 1, pl.ds(0, early), :, pl.ds(start, GROUP), columns],
            dst_ref=owned.at[
                pl.ds(0, early), :, pl.ds(pl.multiple_of(me * blocks + start, GROUP), GROUP), columns
            ],
            send_sem=early_sem.at[0],
            recv_sem=early_sem.at[1],
            device_id={"tm": partner(me, k, n_tm)},
            device_id_type=MESH,
        )

    def later_copy(item, k):
        first, size, column, span = later[item]
        columns = pl.ds(column, span)
        return pltpu.make_async_remote_copy(
            src_ref=outgoing.at[k - 1, pl.ds(first, size), :, :, columns],
            dst_ref=owned.at[pl.ds(first, size), :, pl.ds(pl.multiple_of(me * blocks, GROUP), blocks), columns],
            send_sem=unit_send.at[max(item - (len(later) - SHARES - 2), 0)],
            recv_sem=unit_recv.at[item],
            device_id={"tm": partner(me, k, n_tm)},
            device_id_type=MESH,
        )

    def move_copy(i, k):
        columns = pl.ds(cut + i * share, share)
        mine = pl.ds(pl.multiple_of(me * blocks, GROUP), blocks)
        if k:
            source = outgoing.at[k - 1, pl.ds(last_first, unit_size), :, :, columns]
            target = spare_out.at[i, k - 1]
        else:
            source = owned.at[pl.ds(last_first, unit_size), :, mine, columns]
            target = spare.at[i, :, :, mine]
        return pltpu.make_async_remote_copy(
            src_ref=source,
            dst_ref=target,
            send_sem=move_send.at[i],
            recv_sem=move_recv.at[i],
            device_id={"space": taker},
            device_id_type=MESH,
        )

    def spare_copy(i, k):
        return pltpu.make_async_remote_copy(
            src_ref=spare_out.at[i, k - 1],
            dst_ref=spare.at[i, :, :, pl.ds(pl.multiple_of(me * blocks, GROUP), blocks)],
            send_sem=spare_send.at[i],
            recv_sem=spare_recv.at[i],
            device_id={"tm": partner(me, k, n_tm)},
            device_id_type=MESH,
        )

    def sum_copy(unit, k):
        owner = partner(seat, k, n_space)
        group = sum([jnp.where(unit >= low, 1, 0) for low, _ in groups[1:]])
        return pltpu.make_async_remote_copy(
            src_ref=part.at[unit, owner],
            dst_ref=arrived.at[unit, k - 1],
            send_sem=sum_send.at[0],
            recv_sem=sum_recv.at[group],
            device_id={"space": owner},
            device_id_type=MESH,
        )

    first, rest = row_order(n_tm, freqs, early)
    place_of = {pair: i for i, pair in enumerate(first + rest)}
    split = len(first) * 2 * GROUP
    def wait_bytes(ref, semaphore):
        pltpu.make_async_copy(ref, ref, semaphore).wait()

    def later_part(item):
        item_first, size, column, span = later[item]
        return outgoing.at[:, pl.ds(item_first, size), :, :, pl.ds(column, span)]

    constants = [
        pltpu.make_async_copy(pair[0], pair[1], const_sem.at[i])
        for i, pair in enumerate(
            [(table_hbm.at[me], table_ref), (w_hbm, w_ref), (swap_hbm, swap_ref), (order_hbm, order_ref)]
        )
    ]
    load(0, 0).start()
    constants[0].start()
    constants[1].start()
    for q in range(1, GROUP // PART):
        load(0, q).start()
    constants[2].start()
    constants[3].start()
    barrier = pltpu.get_barrier_semaphore()
    core = seat + 1 - 2 * lax.rem(seat, 2)
    met = len(peers) + 1 + (seat >= 2).astype(jnp.int32) + (seat + 2 < n_space).astype(jnp.int32)

    def greet(semaphore):
        for k in peers:
            pl.semaphore_signal(semaphore, inc=1, device_id={"tm": partner(me, k, n_tm)}, device_id_type=MESH)
        pl.semaphore_signal(semaphore, inc=1, device_id={"space": core}, device_id_type=MESH)

        @pl.when(seat >= 2)
        def _():
            pl.semaphore_signal(semaphore, inc=1, device_id={"space": seat - 2}, device_id_type=MESH)

        @pl.when(seat + 2 < n_space)
        def _():
            pl.semaphore_signal(semaphore, inc=1, device_id={"space": seat + 2}, device_id_type=MESH)

    greet(barrier)
    for copy in constants[:2]:
        copy.wait()

    def transform(step, carry):
        start, column = place(step)

        @pl.when(step + 1 < steps)
        def _():
            for q in range(GROUP // PART):
                load(step + 1, q).start()

        scale = jnp.sqrt(w_ref[:, pl.ds(column, width)])

        def product(b, low, high):
            value = jnp.dot(table_ref[low:high], x_buf[step % 2, b], preferred_element_type=jnp.float32)
            rows_buf[b, low:high] = (value * scale).astype(jnp.bfloat16)

        def exchange(k, f):
            target = owned if k == 0 else outgoing.at[k - 1]
            offset = me * blocks + start if k == 0 else start
            for c in range(2):
                row = (2 * place_of[k, f] + c) * GROUP
                taken = rows_buf[:, row : row + GROUP, :].reshape(GROUP * GROUP, width)
                swapped = jnp.dot(swap_ref[...], taken, preferred_element_type=jnp.float32)
                target[
                    pl.ds(f, GROUP), c, pl.ds(pl.multiple_of(offset, GROUP), GROUP), pl.ds(column, width)
                ] = swapped.astype(jnp.bfloat16).reshape(GROUP, GROUP, width)

        for q in range(GROUP // PART):
            load(step, q).wait()
            for b in range(q * PART, (q + 1) * PART):
                product(b, 0, split)
        @pl.when(step == 0)
        def _():
            for copy in constants[2:]:
                copy.wait()

        for k, f in first:
            exchange(k, f)

        @pl.when(step == 0)
        def _():
            pl.semaphore_wait(barrier, met)
            if rounds > 1:
                greet(round_sem.at[0])

        for item in range(len(batches)):

            @pl.when(step == batches[item][0])
            def _(item=item):
                for k in peers:
                    early_copy(item, k).start()

        def second(b, inner):
            product(b, split, length)
            return inner

        lax.fori_loop(0, GROUP, second, 0, unroll=16)
        for k, f in rest:
            exchange(k, f)
        return carry

    lax.fori_loop(0, steps, transform, 0)

    def meet(r, carry):
        pl.semaphore_wait(round_sem.at[r - 1], met)

        @pl.when(r + 1 < rounds)
        def _():
            greet(round_sem.at[r])

        return carry

    lax.fori_loop(1, rounds, meet, 0)

    if moving(n_space):
        for i in range(SHARES):

            @pl.when(gives[i])
            def _(i=i):
                for k in range(n_tm):
                    move_copy(i, k).start()

        for i in range(SHARES):

            @pl.when(takes[i])
            def _(i=i):
                wait_bytes(spare.at[i], move_recv.at[i])
                for k in peers:
                    spare_copy(i, k).start()

            @pl.when(jnp.logical_not(takes[i]))
            def _(i=i):
                spare[i] = jnp.zeros(spare.shape[1:], jnp.bfloat16)

            @pl.when(gives[i])
            def _(i=i):
                wait_bytes(spare.at[i], move_send.at[i])
                owned[last_first:, :, :, cut + i * share : cut + (i + 1) * share] = jnp.zeros(
                    (unit_size, 2, total, share), jnp.bfloat16
                )

    def own_shares(act):
        for i in range(SHARES):

            @pl.when(jnp.logical_not(gives[i]) if moving(n_space) else True)
            def _(i=i):
                act(i, len(later) - SHARES + i)

    def spare_shares(semaphores):
        if moving(n_space):
            for i in range(SHARES):

                @pl.when(takes[i])
                def _(i=i):
                    wait_bytes(spare_out.at[i], semaphores.at[i])

    def start_later(item):
        for k in peers:
            later_copy(item, k).start()

    for item in range(len(later) - SHARES):
        start_later(item)
    own_shares(lambda i, item: start_later(item))

    wait_bytes(outgoing.at[:, pl.ds(0, early)], early_sem.at[1])

    def finish(unit):
        value = part[unit, seat].astype(jnp.float32)
        for k in range(n_space - 1):
            value = value + arrived[unit, k].astype(jnp.float32)
        for i in range(2 * unit_size):
            out_buf[:, pl.ds(unit * 2 * unit_size + i, 1), :] = value[i * rows : (i + 1) * rows][:, None, :]

    def finish_group(g):
        low, size = groups[g]
        wait_bytes(arrived.at[pl.ds(low, size)], sum_recv.at[g])

        def one(unit, carry):
            finish(unit)
            return carry

        if size == 1:
            finish(low)
        else:
            lax.fori_loop(low, low + size, one, 0)

    def cross(unit, last):
        for item in range(len(later) - SHARES):
            if last:
                if item == len(later) - SHARES - 1:
                    wait_bytes(later_part(item), unit_recv.at[item])
            elif item < len(later) - SHARES - 1:

                @pl.when(unit == later[item][0] // unit_size)
                def _(item=item):
                    wait_bytes(later_part(item), unit_recv.at[item])

        pieces = []
        grams = []
        middle = cut if last else points // 2
        for low, high in ((0, middle), (middle, points)):
            if low and last:
                spare_shares(spare_recv)
                own_shares(lambda i, item: wait_bytes(later_part(item), unit_recv.at[item]))
            for i in range(unit_size):
                both = owned[unit * unit_size + i, :, :, pl.ds(low, high - low)].reshape(2 * total, high - low)
                if low and last and moving(n_space):
                    extra = [spare[j, i].reshape(2 * total, share) for j in range(SHARES)]
                    both = jnp.concatenate([both] + extra, axis=1)
                grams.append(
                    lax.dot_general(both, both, (((1,), (1,)), ((), ())), preferred_element_type=jnp.float32)
                )
        for i in range(unit_size):
            gram = grams[i] + grams[unit_size + i]
            pieces.append(gram[:total, :total] + gram[total:, total:])
            pieces.append(gram[:total, total:] - gram[total:, :total])
        pieces = [piece.astype(jnp.bfloat16) for piece in pieces]
        if rows % GROUP == 0:
            for i, piece in enumerate(pieces):
                for d in range(n_space):
                    part[unit, d, i * rows : (i + 1) * rows, :] = piece[d * rows : (d + 1) * rows]
        else:
            ordered = jnp.dot(
                order_ref[...], jnp.concatenate(pieces, axis=0), preferred_element_type=jnp.float32
            )
            part[unit] = ordered.astype(jnp.bfloat16).reshape(n_space, slab, total)

        for k in seats:
            sum_copy(unit, k).start()

        if not last:
            for g, (low, size) in enumerate(groups):
                if low + size + 1 < units - 1:

                    @pl.when(unit == low + size + 1)
                    def _(g=g):
                        finish_group(g)

    def cross_step(unit, carry):
        cross(unit, False)
        return carry

    lax.fori_loop(0, units - 1, cross_step, 0)
    cross(units - 1, True)
    for g, (low, size) in enumerate(groups):
        if low + size + 1 >= units - 1:
            finish_group(g)

    wait_bytes(arrived, sum_send.at[0])
    wait_bytes(outgoing.at[:, pl.ds(0, early)], early_sem.at[0])
    wait_bytes(outgoing.at[:, pl.ds(early, last_first - early)], unit_send.at[0])
    wait_bytes(later_part(len(later) - SHARES - 1), unit_send.at[1])
    spare_shares(spare_send)
    own_shares(lambda i, item: wait_bytes(later_part(item), unit_send.at[2 + i]))


def per_device(n_tm, n_space, snapshots, weights):
    blocks, length, points = snapshots.shape
    total, freqs = blocks * n_tm, length // 2 // n_tm
    rows = total // n_space
    unit_size = max(1, GROUP // (2 * rows))
    units = freqs // unit_size
    slab = unit_size * 2 * rows
    width = min(WIDTH, points)
    early = max(freqs // 2, unit_size)
    later, first = [], early
    while first + unit_size < freqs:
        size = max(unit_size, (freqs - first) // (2 * unit_size) * unit_size)
        later.append((first, size, 0, points))
        first += size
    moved = points // 4
    share = moved // SHARES
    later.append((first, unit_size, 0, points - moved))
    later += [(first, unit_size, points - moved + i * share, share) for i in range(SHARES)]
    batches = early_batches(blocks, points, width)
    groups, low = [], 0
    while low < units:
        groups.append((low, max(1, (units - low) // 2)))
        low += groups[-1][1]
    hbm = pl.BlockSpec(memory_space=pl.ANY)
    bf16 = jnp.bfloat16
    table = ordered_tables(make_table(length, length // 2), n_tm, freqs, early)
    swap = swap_matrix()
    order = swap if rows % GROUP == 0 else order_matrix(unit_size, total, n_space)
    sums = pl.pallas_call(
        functools.partial(kernel, n_tm, n_space, width, early, unit_size, batches, later, groups),
        out_shape=pltpu.VMEM((rows, freqs * 2, total), jnp.float32),
        in_specs=[hbm] * 5,
        out_specs=pl.BlockSpec(memory_space=pltpu.VMEM),
        scratch_shapes=[
            pltpu.VMEM((1, points), jnp.float32),
            pltpu.VMEM(table.shape[1:], bf16),
            pltpu.VMEM(swap.shape, bf16),
            pltpu.VMEM(order.shape, bf16),
            pltpu.VMEM((2, GROUP, length, width), bf16),
            pltpu.VMEM((GROUP, length, width), bf16),
            pltpu.VMEM((n_tm - 1, freqs, 2, blocks, points), bf16),
            pltpu.VMEM((freqs, 2, total, points), bf16),
            pltpu.VMEM((units, n_space, slab, total), bf16),
            pltpu.VMEM((units, n_space - 1, slab, total), bf16),
            pltpu.VMEM((SHARES, n_tm - 1, unit_size, 2, blocks, share), bf16),
            pltpu.VMEM((SHARES, unit_size, 2, total, share), bf16),
            pltpu.SemaphoreType.DMA((4,)),
            pltpu.SemaphoreType.DMA((2, GROUP // PART)),
            pltpu.SemaphoreType.DMA((2,)),
            pltpu.SemaphoreType.DMA((2 + SHARES,)),
            pltpu.SemaphoreType.DMA((len(later),)),
            pltpu.SemaphoreType.DMA((1,)),
            pltpu.SemaphoreType.DMA((len(groups),)),
            pltpu.SemaphoreType.REGULAR((max(n_space // 2 - 1, 1),)),
            pltpu.SemaphoreType.DMA((SHARES,)),
            pltpu.SemaphoreType.DMA((SHARES,)),
            pltpu.SemaphoreType.DMA((SHARES,)),
            pltpu.SemaphoreType.DMA((SHARES,)),
        ],
        compiler_params=pltpu.CompilerParams(
            collective_id=0, has_side_effects=True, vmem_limit_bytes=60 * 1024 * 1024
        ),
    )(
        snapshots,
        weights[None, :],
        table,
        swap,
        order,
    )
    return sums.reshape(rows, freqs, 2, total)


def solution(mesh):
    return jax.shard_map(
        functools.partial(per_device, mesh.shape["tm"], mesh.shape["space"]),
        mesh=mesh,
        in_specs=(P("tm", None, "space"), P("space")),
        out_specs=P("space", "tm", None, None),
        check_vma=False,
    )
```

```python
import functools
import math

import jax
import jax.numpy as jnp
import numpy as np
from jax import lax
from jax.experimental import pallas as pl
from jax.experimental.pallas import tpu as pltpu
from jax.sharding import PartitionSpec as P

MESH = pl.DeviceIdType.MESH
WIDTH = 128
GROUP = 16
PART = 8
SHARES = 2


def make_table(length, count):
    steps_t = np.arange(length, dtype=np.int32)
    freqs = np.arange(count, dtype=np.int32)
    turn = np.float32(2.0 * math.pi / length)
    phase = (freqs[:, None] * steps_t[None, :] % length).astype(np.float32) * turn
    hann = np.float32(0.5) - np.float32(0.5) * np.cos(steps_t.astype(np.float32) * turn)
    factor = np.float32(1.0 / math.sqrt(3.0 * length / 8.0))
    table = np.concatenate([np.cos(phase), -np.sin(phase)], axis=0) * hann[None, :] * factor
    return table.astype(jnp.bfloat16)


def swap_matrix():
    size = GROUP * GROUP
    source = np.arange(size).reshape(GROUP, GROUP).T.reshape(-1)
    return jnp.asarray(np.eye(size, dtype=np.float32)[source].astype(jnp.bfloat16))


def order_matrix(unit_size, blocks, n_space):
    size = unit_size * 2 * blocks
    rows = blocks // n_space
    source = np.arange(size).reshape(unit_size, 2, n_space, rows).transpose(2, 0, 1, 3).reshape(-1)
    return jnp.asarray(np.eye(size, dtype=np.float32)[source].astype(jnp.bfloat16))


def partner(me, k, count):
    if count & (count - 1):
        return lax.rem(me + k, count)
    other, bit = 0, 1
    while bit < count:
        have = lax.rem(lax.div(me, bit), 2)
        other = other + bit * (1 - have if k & bit else have)
        bit *= 2
    return other


def early_batches(blocks, points, width):
    tiles = points // width
    batches = []
    for group in range(blocks // GROUP):
        tile = 0
        while tile < tiles:
            count = tiles if group else max(tile, 1)
            count = min(count, tiles - tile)
            batches.append((group * tiles + tile + count - 1, group * GROUP, tile * width, count * width))
            tile += count
    return batches


def moving(n_space):
    return n_space >= 8


def row_order(n_tm, freqs, early):
    peers = range(n_tm - 1, 0, -1)
    starts = range(0, freqs, GROUP)
    first = [(k, f) for f in starts if f < early for k in peers]
    rest = [(k, f) for f in starts if f >= early for k in peers] + [(0, f) for f in starts]
    return first, rest


def ordered_tables(table, n_tm, freqs, early):
    first, rest = row_order(n_tm, freqs, early)
    tables = []
    for me in range(n_tm):
        owners = [((me + k) % n_tm if n_tm & (n_tm - 1) else me ^ k, f) for k, f in first + rest]
        rows = [c * n_tm * freqs + owner * freqs + f + np.arange(GROUP) for owner, f in owners for c in range(2)]
        tables.append(table[np.concatenate(rows)])
    return jnp.asarray(np.stack(tables))


def kernel(
    n_tm, n_space, width, early, unit_size, batches, later, groups,
    x_ref, w_hbm, table_hbm, swap_hbm, order_hbm, out_buf,
    w_ref, table_ref, swap_ref, order_ref,
    x_buf, rows_buf, outgoing, owned, part, arrived, spare_out, spare,
    const_sem, x_sem, early_sem, unit_send, unit_recv, sum_send, sum_recv, round_sem,
    move_send, move_recv, spare_send, spare_recv,
):
    me = lax.axis_index("tm")
    seat = lax.axis_index("space")
    blocks, length, points = x_ref.shape
    half = length // 2
    freqs = half // n_tm
    tiles = points // width
    steps = blocks // GROUP * tiles
    units = freqs // unit_size
    total = blocks * n_tm
    rows = total // n_space
    slab = unit_size * 2 * rows
    peers = list(range(n_tm - 1, 0, -1))
    rounds = n_space // 2
    moved = SHARES * spare.shape[-1]
    cut = points - moved
    last_first = freqs - unit_size
    share = moved // SHARES
    gives = [seat >= n_space - 2, seat >= n_space - 4]
    takes = [seat < 2, seat < 4]
    taker = jnp.where(gives[0], seat - (n_space - 2), seat - (n_space - 6))
    seats = list(range(n_space - 1, 0, -1))

    def place(step):
        start = pl.multiple_of(step // tiles * GROUP, GROUP)
        return start, pl.multiple_of(step % tiles * width, width)

    def load(step, part):
        start, column = place(step)
        return pltpu.make_async_copy(
            x_ref.at[pl.ds(start + part * PART, PART), :, pl.ds(column, width)],
            x_buf.at[step % 2, pl.ds(part * PART, PART)],
            x_sem.at[step % 2, part],
        )

    def early_copy(item, k):
        _, start, column, span = batches[item]
        columns = pl.ds(column, span)
        return pltpu.make_async_remote_copy(
            src_ref=outgoing.at[k - 1, pl.ds(0, early), :, pl.ds(start, GROUP), columns],
            dst_ref=owned.at[
                pl.ds(0, early), :, pl.ds(pl.multiple_of(me * blocks + start, GROUP), GROUP), columns
            ],
            send_sem=early_sem.at[0],
            recv_sem=early_sem.at[1],
            device_id={"tm": partner(me, k, n_tm)},
            device_id_type=MESH,
        )

    def later_copy(item, k):
        first, size, column, span = later[item]
        columns = pl.ds(column, span)
        return pltpu.make_async_remote_copy(
            src_ref=outgoing.at[k - 1, pl.ds(first, size), :, :, columns],
            dst_ref=owned.at[pl.ds(first, size), :, pl.ds(pl.multiple_of(me * blocks, GROUP), blocks), columns],
            send_sem=unit_send.at[max(item - (len(later) - SHARES - 2), 0)],
            recv_sem=unit_recv.at[item],
            device_id={"tm": partner(me, k, n_tm)},
            device_id_type=MESH,
        )

    def move_copy(i, k):
        columns = pl.ds(cut + i * share, share)
        mine = pl.ds(pl.multiple_of(me * blocks, GROUP), blocks)
        if k:
            source = outgoing.at[k - 1, pl.ds(last_first, unit_size), :, :, columns]
            target = spare_out.at[i, k - 1]
        else:
            source = owned.at[pl.ds(last_first, unit_size), :, mine, columns]
            target = spare.at[i, :, :, mine]
        return pltpu.make_async_remote_copy(
            src_ref=source,
            dst_ref=target,
            send_sem=move_send.at[i],
            recv_sem=move_recv.at[i],
            device_id={"space": taker},
            device_id_type=MESH,
        )

    def spare_copy(i, k):
        return pltpu.make_async_remote_copy(
            src_ref=spare_out.at[i, k - 1],
            dst_ref=spare.at[i, :, :, pl.ds(pl.multiple_of(me * blocks, GROUP), blocks)],
            send_sem=spare_send.at[i],
            recv_sem=spare_recv.at[i],
            device_id={"tm": partner(me, k, n_tm)},
            device_id_type=MESH,
        )

    def sum_copy(unit, k):
        owner = partner(seat, k, n_space)
        group = sum([jnp.where(unit >= low, 1, 0) for low, _ in groups[1:]])
        return pltpu.make_async_remote_copy(
            src_ref=part.at[unit, owner],
            dst_ref=arrived.at[unit, k - 1],
            send_sem=sum_send.at[0],
            recv_sem=sum_recv.at[group],
            device_id={"space": owner},
            device_id_type=MESH,
        )

    first, rest = row_order(n_tm, freqs, early)
    place_of = {pair: i for i, pair in enumerate(first + rest)}
    split = len(first) * 2 * GROUP
    def wait_bytes(ref, semaphore):
        pltpu.make_async_copy(ref, ref, semaphore).wait()

    def later_part(item):
        item_first, size, column, span = later[item]
        return outgoing.at[:, pl.ds(item_first, size), :, :, pl.ds(column, span)]

    constants = [
        pltpu.make_async_copy(pair[0], pair[1], const_sem.at[i])
        for i, pair in enumerate(
            [(table_hbm.at[me], table_ref), (w_hbm, w_ref), (swap_hbm, swap_ref)]
            + ([(order_hbm, order_ref)] if rows % GROUP else [])
        )
    ]
    barrier = pltpu.get_barrier_semaphore()
    core = seat + 1 - 2 * lax.rem(seat, 2)
    met = len(peers) + 1 + (seat >= 2).astype(jnp.int32) + (seat + 2 < n_space).astype(jnp.int32)

    def greet(semaphore):
        for k in peers:
            pl.semaphore_signal(semaphore, inc=1, device_id={"tm": partner(me, k, n_tm)}, device_id_type=MESH)
        pl.semaphore_signal(semaphore, inc=1, device_id={"space": core}, device_id_type=MESH)

        @pl.when(seat >= 2)
        def _():
            pl.semaphore_signal(semaphore, inc=1, device_id={"space": seat - 2}, device_id_type=MESH)

        @pl.when(seat + 2 < n_space)
        def _():
            pl.semaphore_signal(semaphore, inc=1, device_id={"space": seat + 2}, device_id_type=MESH)

    greet(barrier)
    load(0, 0).start()
    constants[0].start()
    constants[1].start()
    for q in range(1, GROUP // PART):
        load(0, q).start()
    constants[2].start()
    if rows % GROUP:
        constants[3].start()
    for copy in constants[:2]:
        copy.wait()

    def transform(step, carry):
        start, column = place(step)

        @pl.when(step + 1 < steps)
        def _():
            for q in range(GROUP // PART):
                load(step + 1, q).start()

        scale = jnp.sqrt(w_ref[:, pl.ds(column, width)])

        def product(b, low, high):
            value = jnp.dot(table_ref[low:high], x_buf[step % 2, b], preferred_element_type=jnp.float32)
            rows_buf[b, low:high] = (value * scale).astype(jnp.bfloat16)

        def exchange(k, f):
            target = owned if k == 0 else outgoing.at[k - 1]
            offset = me * blocks + start if k == 0 else start
            for c in range(2):
                row = (2 * place_of[k, f] + c) * GROUP
                taken = rows_buf[:, row : row + GROUP, :].reshape(GROUP * GROUP, width)
                swapped = jnp.dot(swap_ref[...], taken, preferred_element_type=jnp.float32)
                target[
                    pl.ds(f, GROUP), c, pl.ds(pl.multiple_of(offset, GROUP), GROUP), pl.ds(column, width)
                ] = swapped.astype(jnp.bfloat16).reshape(GROUP, GROUP, width)

        for q in range(GROUP // PART):
            load(step, q).wait()
            for b in range(q * PART, (q + 1) * PART):
                product(b, 0, split)
        @pl.when(step == 0)
        def _():
            for copy in constants[2:]:
                copy.wait()

        for k in peers:
            for owner, f in first:
                if owner == k:
                    exchange(k, f)
            if k == peers[0]:

                @pl.when(step == 0)
                def _():
                    pl.semaphore_wait(barrier, met)
                    if rounds > 1:
                        greet(round_sem.at[0])

            for item in range(len(batches)):

                @pl.when(step == batches[item][0])
                def _(item=item, k=k):
                    early_copy(item, k).start()

        def second(b, inner):
            product(b, split, length)
            return inner

        lax.fori_loop(0, GROUP, second, 0, unroll=16)
        for k, f in rest:
            exchange(k, f)
        return carry

    lax.fori_loop(0, steps, transform, 0)

    def meet(r, carry):
        pl.semaphore_wait(round_sem.at[r - 1], met)

        @pl.when(r + 1 < rounds)
        def _():
            greet(round_sem.at[r])

        return carry

    lax.fori_loop(1, rounds, meet, 0)

    if moving(n_space):
        for i in range(SHARES):

            @pl.when(gives[i])
            def _(i=i):
                for k in range(n_tm):
                    move_copy(i, k).start()

        for i in range(SHARES):

            @pl.when(takes[i])
            def _(i=i):
                wait_bytes(spare.at[i], move_recv.at[i])
                for k in peers:
                    spare_copy(i, k).start()

            @pl.when(jnp.logical_not(takes[i]))
            def _(i=i):
                spare[i] = jnp.zeros(spare.shape[1:], jnp.bfloat16)

            @pl.when(gives[i])
            def _(i=i):
                wait_bytes(spare.at[i], move_send.at[i])
                owned[last_first:, :, :, cut + i * share : cut + (i + 1) * share] = jnp.zeros(
                    (unit_size, 2, total, share), jnp.bfloat16
                )

    def own_shares(act):
        for i in range(SHARES):

            @pl.when(jnp.logical_not(gives[i]) if moving(n_space) else True)
            def _(i=i):
                act(i, len(later) - SHARES + i)

    def spare_shares(semaphores):
        if moving(n_space):
            for i in range(SHARES):

                @pl.when(takes[i])
                def _(i=i):
                    wait_bytes(spare_out.at[i], semaphores.at[i])

    def start_later(item):
        for k in peers:
            later_copy(item, k).start()

    for item in range(len(later) - SHARES):
        start_later(item)
    own_shares(lambda i, item: start_later(item))

    wait_bytes(outgoing.at[:, pl.ds(0, early)], early_sem.at[1])

    def finish(unit):
        value = part[unit, seat].astype(jnp.float32)
        for k in range(n_space - 1):
            value = value + arrived[unit, k].astype(jnp.float32)
        for i in range(2 * unit_size):
            out_buf[:, pl.ds(unit * 2 * unit_size + i, 1), :] = value[i * rows : (i + 1) * rows][:, None, :]

    def finish_group(g):
        low, size = groups[g]
        wait_bytes(arrived.at[pl.ds(low, size)], sum_recv.at[g])

        def one(unit, carry):
            finish(unit)
            return carry

        if size == 1:
            finish(low)
        else:
            lax.fori_loop(low, low + size, one, 0)

    def cross(unit, last):
        for item in range(len(later) - SHARES):
            if last:
                if item == len(later) - SHARES - 1:
                    wait_bytes(later_part(item), unit_recv.at[item])
            elif item < len(later) - SHARES - 1:

                @pl.when(unit == later[item][0] // unit_size)
                def _(item=item):
                    wait_bytes(later_part(item), unit_recv.at[item])

        pieces = []
        grams = []
        middle = cut if last else points // 2
        if last:
            spare_shares(spare_recv)
        for low, high in ((0, middle), (middle, points)):
            if low and last:
                own_shares(lambda i, item: wait_bytes(later_part(item), unit_recv.at[item]))
            for i in range(unit_size):
                both = owned[unit * unit_size + i, :, :, pl.ds(low, high - low)].reshape(2 * total, high - low)
                if not low and last and moving(n_space):
                    extra = [spare[j, i].reshape(2 * total, share) for j in range(SHARES)]
                    both = jnp.concatenate([both] + extra, axis=1)
                grams.append(
                    lax.dot_general(both, both, (((1,), (1,)), ((), ())), preferred_element_type=jnp.float32)
                )
        for i in range(unit_size):
            gram = grams[i] + grams[unit_size + i]
            pieces.append(gram[:total, :total] + gram[total:, total:])
            pieces.append(gram[:total, total:] - gram[total:, :total])
        pieces = [piece.astype(jnp.bfloat16) for piece in pieces]
        if rows % GROUP == 0:
            for i, piece in enumerate(pieces):
                for d in range(n_space):
                    part[unit, d, i * rows : (i + 1) * rows, :] = piece[d * rows : (d + 1) * rows]
        else:
            ordered = jnp.dot(
                order_ref[...], jnp.concatenate(pieces, axis=0), preferred_element_type=jnp.float32
            )
            part[unit] = ordered.astype(jnp.bfloat16).reshape(n_space, slab, total)

        for k in seats:
            sum_copy(unit, k).start()

        if not last:
            for g, (low, size) in enumerate(groups):
                if low + size + 1 < units - 1:

                    @pl.when(unit == low + size + 1)
                    def _(g=g):
                        finish_group(g)

    def cross_step(unit, carry):
        cross(unit, False)
        return carry

    lax.fori_loop(0, units - 1, cross_step, 0)
    cross(units - 1, True)
    for g, (low, size) in enumerate(groups):
        if low + size + 1 >= units - 1:
            finish_group(g)

    wait_bytes(arrived, sum_send.at[0])
    wait_bytes(outgoing.at[:, pl.ds(0, early)], early_sem.at[0])
    wait_bytes(outgoing.at[:, pl.ds(early, last_first - early)], unit_send.at[0])
    wait_bytes(later_part(len(later) - SHARES - 1), unit_send.at[1])
    spare_shares(spare_send)
    own_shares(lambda i, item: wait_bytes(later_part(item), unit_send.at[2 + i]))


def per_device(n_tm, n_space, snapshots, weights):
    blocks, length, points = snapshots.shape
    total, freqs = blocks * n_tm, length // 2 // n_tm
    rows = total // n_space
    unit_size = max(1, GROUP // (2 * rows))
    units = freqs // unit_size
    slab = unit_size * 2 * rows
    width = min(WIDTH, points)
    early = max(freqs // 2, unit_size)
    later, first = [], early
    while first + unit_size < freqs:
        size = max(unit_size, (freqs - first) // (2 * unit_size) * unit_size)
        later.append((first, size, 0, points))
        first += size
    moved = points // 4
    share = moved // SHARES
    later.append((first, unit_size, 0, points - moved))
    later += [(first, unit_size, points - moved + i * share, share) for i in range(SHARES)]
    batches = early_batches(blocks, points, width)
    groups, low = [], 0
    while low < units:
        groups.append((low, max(1, (units - low) // 2)))
        low += groups[-1][1]
    hbm = pl.BlockSpec(memory_space=pl.ANY)
    bf16 = jnp.bfloat16
    table = ordered_tables(make_table(length, length // 2), n_tm, freqs, early)
    swap = swap_matrix()
    order = swap if rows % GROUP == 0 else order_matrix(unit_size, total, n_space)
    sums = pl.pallas_call(
        functools.partial(kernel, n_tm, n_space, width, early, unit_size, batches, later, groups),
        out_shape=pltpu.VMEM((rows, freqs * 2, total), jnp.float32),
        in_specs=[hbm] * 5,
        out_specs=pl.BlockSpec(memory_space=pltpu.VMEM),
        scratch_shapes=[
            pltpu.VMEM((1, points), jnp.float32),
            pltpu.VMEM(table.shape[1:], bf16),
            pltpu.VMEM(swap.shape, bf16),
            pltpu.VMEM(order.shape, bf16),
            pltpu.VMEM((2, GROUP, length, width), bf16),
            pltpu.VMEM((GROUP, length, width), bf16),
            pltpu.VMEM((n_tm - 1, freqs, 2, blocks, points), bf16),
            pltpu.VMEM((freqs, 2, total, points), bf16),
            pltpu.VMEM((units, n_space, slab, total), bf16),
            pltpu.VMEM((units, n_space - 1, slab, total), bf16),
            pltpu.VMEM((SHARES, n_tm - 1, unit_size, 2, blocks, share), bf16),
            pltpu.VMEM((SHARES, unit_size, 2, total, share), bf16),
            pltpu.SemaphoreType.DMA((4,)),
            pltpu.SemaphoreType.DMA((2, GROUP // PART)),
            pltpu.SemaphoreType.DMA((2,)),
            pltpu.SemaphoreType.DMA((2 + SHARES,)),
            pltpu.SemaphoreType.DMA((len(later),)),
            pltpu.SemaphoreType.DMA((1,)),
            pltpu.SemaphoreType.DMA((len(groups),)),
            pltpu.SemaphoreType.REGULAR((max(n_space // 2 - 1, 1),)),
            pltpu.SemaphoreType.DMA((SHARES,)),
            pltpu.SemaphoreType.DMA((SHARES,)),
            pltpu.SemaphoreType.DMA((SHARES,)),
            pltpu.SemaphoreType.DMA((SHARES,)),
        ],
        compiler_params=pltpu.CompilerParams(
            collective_id=0, has_side_effects=True, vmem_limit_bytes=60 * 1024 * 1024
        ),
    )(
        snapshots,
        weights[None, :],
        table,
        swap,
        order,
    )
    return sums.reshape(rows, freqs, 2, total)


def solution(mesh):
    return jax.shard_map(
        functools.partial(per_device, mesh.shape["tm"], mesh.shape["space"]),
        mesh=mesh,
        in_specs=(P("tm", None, "space"), P("space")),
        out_specs=P("space", "tm", None, None),
        check_vma=False,
    )
```

```python
import functools
import math

import jax
import jax.numpy as jnp
import numpy as np
from jax import lax
from jax.experimental import pallas as pl
from jax.experimental.pallas import tpu as pltpu
from jax.sharding import PartitionSpec as P

MESH = pl.DeviceIdType.MESH
WIDTH = 128
GROUP = 16
PART = 8
SHARES = 2


def make_table(length, count):
    steps_t = np.arange(length, dtype=np.int32)
    freqs = np.arange(count, dtype=np.int32)
    turn = np.float32(2.0 * math.pi / length)
    phase = (freqs[:, None] * steps_t[None, :] % length).astype(np.float32) * turn
    hann = np.float32(0.5) - np.float32(0.5) * np.cos(steps_t.astype(np.float32) * turn)
    factor = np.float32(1.0 / math.sqrt(3.0 * length / 8.0))
    table = np.concatenate([np.cos(phase), -np.sin(phase)], axis=0) * hann[None, :] * factor
    return table.astype(jnp.bfloat16)


def swap_matrix():
    size = GROUP * GROUP
    source = np.arange(size).reshape(GROUP, GROUP).T.reshape(-1)
    return jnp.asarray(np.eye(size, dtype=np.float32)[source].astype(jnp.bfloat16))


def order_matrix(unit_size, blocks, n_space):
    size = unit_size * 2 * blocks
    rows = blocks // n_space
    source = np.arange(size).reshape(unit_size, 2, n_space, rows).transpose(2, 0, 1, 3).reshape(-1)
    return jnp.asarray(np.eye(size, dtype=np.float32)[source].astype(jnp.bfloat16))


def partner(me, k, count):
    if count & (count - 1):
        return lax.rem(me + k, count)
    other, bit = 0, 1
    while bit < count:
        have = lax.rem(lax.div(me, bit), 2)
        other = other + bit * (1 - have if k & bit else have)
        bit *= 2
    return other


def early_batches(blocks, points, width):
    tiles = points // width
    batches = []
    for group in range(blocks // GROUP):
        tile = 0
        while tile < tiles:
            count = tiles if group else max(tile, 1)
            count = min(count, tiles - tile)
            batches.append((group * tiles + tile + count - 1, group * GROUP, tile * width, count * width))
            tile += count
    return batches


def moving(n_space):
    return n_space >= 8


def row_order(n_tm, freqs, early):
    peers = range(n_tm - 1, 0, -1)
    starts = range(0, freqs, GROUP)
    first = [(k, f) for f in starts if f < early for k in peers]
    rest = [(k, f) for f in starts if f >= early for k in peers] + [(0, f) for f in starts]
    return first, rest


def ordered_tables(table, n_tm, freqs, early):
    first, rest = row_order(n_tm, freqs, early)
    tables = []
    for me in range(n_tm):
        owners = [((me + k) % n_tm if n_tm & (n_tm - 1) else me ^ k, f) for k, f in first + rest]
        rows = [c * n_tm * freqs + owner * freqs + f + np.arange(GROUP) for owner, f in owners for c in range(2)]
        tables.append(table[np.concatenate(rows)])
    return jnp.asarray(np.stack(tables))


def kernel(
    n_tm, n_space, width, early, unit_size, batches, later, groups,
    x_ref, w_hbm, table_hbm, swap_hbm, order_hbm, out_buf,
    w_ref, table_ref, swap_ref, order_ref,
    x_buf, rows_buf, outgoing, owned, part, arrived, spare_out, spare,
    const_sem, x_sem, early_sem, unit_send, unit_recv, sum_send, sum_recv, round_sem,
    move_send, move_recv, spare_send, spare_recv,
):
    me = lax.axis_index("tm")
    seat = lax.axis_index("space")
    blocks, length, points = x_ref.shape
    half = length // 2
    freqs = half // n_tm
    tiles = points // width
    steps = blocks // GROUP * tiles
    units = freqs // unit_size
    total = blocks * n_tm
    rows = total // n_space
    slab = unit_size * 2 * rows
    peers = list(range(n_tm - 1, 0, -1))
    rounds = n_space // 2
    moved = SHARES * spare.shape[-1]
    cut = points - moved
    last_first = freqs - unit_size
    share = moved // SHARES
    gives = [seat >= n_space - 2, seat >= n_space - 4]
    takes = [seat < 2, seat < 4]
    taker = jnp.where(gives[0], seat - (n_space - 2), seat - (n_space - 6))
    seats = list(range(n_space - 1, 0, -1))

    def place(step):
        start = pl.multiple_of(step // tiles * GROUP, GROUP)
        return start, pl.multiple_of(step % tiles * width, width)

    def load(step, part):
        start, column = place(step)
        return pltpu.make_async_copy(
            x_ref.at[pl.ds(start + part * PART, PART), :, pl.ds(column, width)],
            x_buf.at[step % 2, pl.ds(part * PART, PART)],
            x_sem.at[step % 2, part],
        )

    def early_copy(item, k):
        _, start, column, span = batches[item]
        columns = pl.ds(column, span)
        return pltpu.make_async_remote_copy(
            src_ref=outgoing.at[k - 1, pl.ds(0, early), :, pl.ds(start, GROUP), columns],
            dst_ref=owned.at[
                pl.ds(0, early), :, pl.ds(pl.multiple_of(me * blocks + start, GROUP), GROUP), columns
            ],
            send_sem=early_sem.at[0],
            recv_sem=early_sem.at[1],
            device_id={"tm": partner(me, k, n_tm)},
            device_id_type=MESH,
        )

    def later_copy(item, k):
        first, size, column, span = later[item]
        columns = pl.ds(column, span)
        return pltpu.make_async_remote_copy(
            src_ref=outgoing.at[k - 1, pl.ds(first, size), :, :, columns],
            dst_ref=owned.at[pl.ds(first, size), :, pl.ds(pl.multiple_of(me * blocks, GROUP), blocks), columns],
            send_sem=unit_send.at[max(item - (len(later) - SHARES - 2), 0)],
            recv_sem=unit_recv.at[item],
            device_id={"tm": partner(me, k, n_tm)},
            device_id_type=MESH,
        )

    def move_copy(i, k):
        columns = pl.ds(cut + i * share, share)
        mine = pl.ds(pl.multiple_of(me * blocks, GROUP), blocks)
        if k:
            source = outgoing.at[k - 1, pl.ds(last_first, unit_size), :, :, columns]
            target = spare_out.at[i, k - 1]
        else:
            source = owned.at[pl.ds(last_first, unit_size), :, mine, columns]
            target = spare.at[i, :, :, mine]
        return pltpu.make_async_remote_copy(
            src_ref=source,
            dst_ref=target,
            send_sem=move_send.at[i],
            recv_sem=move_recv.at[i],
            device_id={"space": taker},
            device_id_type=MESH,
        )

    def spare_copy(i, k):
        return pltpu.make_async_remote_copy(
            src_ref=spare_out.at[i, k - 1],
            dst_ref=spare.at[i, :, :, pl.ds(pl.multiple_of(me * blocks, GROUP), blocks)],
            send_sem=spare_send.at[i],
            recv_sem=spare_recv.at[i],
            device_id={"tm": partner(me, k, n_tm)},
            device_id_type=MESH,
        )

    def sum_copy(unit, k):
        owner = partner(seat, k, n_space)
        group = sum([jnp.where(unit >= low, 1, 0) for low, _ in groups[1:]])
        return pltpu.make_async_remote_copy(
            src_ref=part.at[unit, owner],
            dst_ref=arrived.at[unit, k - 1],
            send_sem=sum_send.at[0],
            recv_sem=sum_recv.at[group],
            device_id={"space": owner},
            device_id_type=MESH,
        )

    first, rest = row_order(n_tm, freqs, early)
    place_of = {pair: i for i, pair in enumerate(first + rest)}
    split = len(first) * 2 * GROUP
    def wait_bytes(ref, semaphore):
        pltpu.make_async_copy(ref, ref, semaphore).wait()

    def later_part(item):
        item_first, size, column, span = later[item]
        return outgoing.at[:, pl.ds(item_first, size), :, :, pl.ds(column, span)]

    constants = [
        pltpu.make_async_copy(pair[0], pair[1], const_sem.at[i])
        for i, pair in enumerate(
            [(table_hbm.at[me], table_ref), (w_hbm, w_ref), (swap_hbm, swap_ref)]
            + ([(order_hbm, order_ref)] if rows % GROUP else [])
        )
    ]
    barrier = pltpu.get_barrier_semaphore()
    core = seat + 1 - 2 * lax.rem(seat, 2)
    met = len(peers) + 1 + (seat >= 2).astype(jnp.int32) + (seat + 2 < n_space).astype(jnp.int32)

    def greet(semaphore):
        for k in peers:
            pl.semaphore_signal(semaphore, inc=1, device_id={"tm": partner(me, k, n_tm)}, device_id_type=MESH)
        pl.semaphore_signal(semaphore, inc=1, device_id={"space": core}, device_id_type=MESH)

        @pl.when(seat >= 2)
        def _():
            pl.semaphore_signal(semaphore, inc=1, device_id={"space": seat - 2}, device_id_type=MESH)

        @pl.when(seat + 2 < n_space)
        def _():
            pl.semaphore_signal(semaphore, inc=1, device_id={"space": seat + 2}, device_id_type=MESH)

    greet(barrier)
    load(0, 0).start()
    constants[0].start()
    constants[1].start()
    for q in range(1, GROUP // PART):
        load(0, q).start()
    constants[2].start()
    if rows % GROUP:
        constants[3].start()
    for copy in constants[:2]:
        copy.wait()

    def transform(step, carry):
        start, column = place(step)

        @pl.when(step + 1 < steps)
        def _():
            for q in range(GROUP // PART):
                load(step + 1, q).start()

        scale = jnp.sqrt(w_ref[:, pl.ds(column, width)])

        def product(b, low, high):
            value = jnp.dot(table_ref[low:high], x_buf[step % 2, b], preferred_element_type=jnp.float32)
            rows_buf[b, low:high] = (value * scale).astype(jnp.bfloat16)

        def exchange(k, f):
            target = owned if k == 0 else outgoing.at[k - 1]
            offset = me * blocks + start if k == 0 else start
            for c in range(2):
                row = (2 * place_of[k, f] + c) * GROUP
                taken = rows_buf[:, row : row + GROUP, :].reshape(GROUP * GROUP, width)
                swapped = jnp.dot(swap_ref[...], taken, preferred_element_type=jnp.float32)
                target[
                    pl.ds(f, GROUP), c, pl.ds(pl.multiple_of(offset, GROUP), GROUP), pl.ds(column, width)
                ] = swapped.astype(jnp.bfloat16).reshape(GROUP, GROUP, width)

        for q in range(GROUP // PART):
            load(step, q).wait()
            for b in range(q * PART, (q + 1) * PART):
                product(b, 0, split)
        @pl.when(step == 0)
        def _():
            for copy in constants[2:]:
                copy.wait()

        for k in peers:
            for owner, f in first:
                if owner == k:
                    exchange(k, f)
            if k == peers[0]:

                @pl.when(step == 0)
                def _():
                    pl.semaphore_wait(barrier, met)

            for item in range(len(batches)):

                @pl.when(step == batches[item][0])
                def _(item=item, k=k):
                    early_copy(item, k).start()

        if rounds > 1:

            @pl.when(step == 0)
            def _():
                greet(round_sem.at[0])

        def second(b, inner):
            product(b, split, length)
            return inner

        lax.fori_loop(0, GROUP, second, 0, unroll=16)
        for k, f in rest:
            exchange(k, f)
        return carry

    lax.fori_loop(0, steps, transform, 0)

    def meet(r, carry):
        pl.semaphore_wait(round_sem.at[r - 1], met)

        @pl.when(r + 1 < rounds)
        def _():
            greet(round_sem.at[r])

        return carry

    lax.fori_loop(1, rounds, meet, 0)

    if moving(n_space):
        for i in range(SHARES):

            @pl.when(gives[i])
            def _(i=i):
                for k in range(n_tm):
                    move_copy(i, k).start()

        for i in range(SHARES):

            @pl.when(takes[i])
            def _(i=i):
                wait_bytes(spare.at[i], move_recv.at[i])
                for k in peers:
                    spare_copy(i, k).start()

            @pl.when(jnp.logical_not(takes[i]))
            def _(i=i):
                spare[i] = jnp.zeros(spare.shape[1:], jnp.bfloat16)

            @pl.when(gives[i])
            def _(i=i):
                wait_bytes(spare.at[i], move_send.at[i])
                owned[last_first:, :, :, cut + i * share : cut + (i + 1) * share] = jnp.zeros(
                    (unit_size, 2, total, share), jnp.bfloat16
                )

    def own_shares(act):
        for i in range(SHARES):

            @pl.when(jnp.logical_not(gives[i]) if moving(n_space) else True)
            def _(i=i):
                act(i, len(later) - SHARES + i)

    def spare_shares(semaphores):
        if moving(n_space):
            for i in range(SHARES):

                @pl.when(takes[i])
                def _(i=i):
                    wait_bytes(spare_out.at[i], semaphores.at[i])

    def start_later(item):
        for k in peers:
            later_copy(item, k).start()

    for item in range(len(later) - SHARES):
        start_later(item)
    own_shares(lambda i, item: start_later(item))

    wait_bytes(outgoing.at[:, pl.ds(0, early)], early_sem.at[1])

    def finish(unit):
        value = part[unit, seat].astype(jnp.float32)
        for k in range(n_space - 1):
            value = value + arrived[unit, k].astype(jnp.float32)
        for i in range(2 * unit_size):
            out_buf[:, pl.ds(unit * 2 * unit_size + i, 1), :] = value[i * rows : (i + 1) * rows][:, None, :]

    def finish_group(g):
        low, size = groups[g]
        wait_bytes(arrived.at[pl.ds(low, size)], sum_recv.at[g])

        def one(unit, carry):
            finish(unit)
            return carry

        if size == 1:
            finish(low)
        else:
            lax.fori_loop(low, low + size, one, 0)

    def cross(unit, last):
        for item in range(len(later) - SHARES):
            if last:
                if item == len(later) - SHARES - 1:
                    wait_bytes(later_part(item), unit_recv.at[item])
            elif item < len(later) - SHARES - 1:

                @pl.when(unit == later[item][0] // unit_size)
                def _(item=item):
                    wait_bytes(later_part(item), unit_recv.at[item])

        pieces = []
        grams = []
        middle = cut if last else points // 2
        if last:
            spare_shares(spare_recv)
        for low, high in ((0, middle), (middle, points)):
            if low and last:
                own_shares(lambda i, item: wait_bytes(later_part(item), unit_recv.at[item]))
            for i in range(unit_size):
                both = owned[unit * unit_size + i, :, :, pl.ds(low, high - low)].reshape(2 * total, high - low)
                if not low and last and moving(n_space):
                    extra = [spare[j, i].reshape(2 * total, share) for j in range(SHARES)]
                    both = jnp.concatenate([both] + extra, axis=1)
                grams.append(
                    lax.dot_general(both, both, (((1,), (1,)), ((), ())), preferred_element_type=jnp.float32)
                )
        for i in range(unit_size):
            gram = grams[i] + grams[unit_size + i]
            pieces.append(gram[:total, :total] + gram[total:, total:])
            pieces.append(gram[:total, total:] - gram[total:, :total])
        pieces = [piece.astype(jnp.bfloat16) for piece in pieces]
        if rows % GROUP == 0:
            for i, piece in enumerate(pieces):
                for d in range(n_space):
                    part[unit, d, i * rows : (i + 1) * rows, :] = piece[d * rows : (d + 1) * rows]
        else:
            ordered = jnp.dot(
                order_ref[...], jnp.concatenate(pieces, axis=0), preferred_element_type=jnp.float32
            )
            part[unit] = ordered.astype(jnp.bfloat16).reshape(n_space, slab, total)

        for k in seats:
            sum_copy(unit, k).start()

        if not last:
            for g, (low, size) in enumerate(groups):
                if low + size + 1 < units - 1:

                    @pl.when(unit == low + size + 1)
                    def _(g=g):
                        finish_group(g)

    def cross_step(unit, carry):
        cross(unit, False)
        return carry

    lax.fori_loop(0, units - 1, cross_step, 0)
    cross(units - 1, True)
    for g, (low, size) in enumerate(groups):
        if low + size + 1 >= units - 1:
            finish_group(g)

    wait_bytes(arrived, sum_send.at[0])
    wait_bytes(outgoing.at[:, pl.ds(0, early)], early_sem.at[0])
    wait_bytes(outgoing.at[:, pl.ds(early, last_first - early)], unit_send.at[0])
    wait_bytes(later_part(len(later) - SHARES - 1), unit_send.at[1])
    spare_shares(spare_send)
    own_shares(lambda i, item: wait_bytes(later_part(item), unit_send.at[2 + i]))


def per_device(n_tm, n_space, snapshots, weights):
    blocks, length, points = snapshots.shape
    total, freqs = blocks * n_tm, length // 2 // n_tm
    rows = total // n_space
    unit_size = max(1, GROUP // (2 * rows))
    units = freqs // unit_size
    slab = unit_size * 2 * rows
    width = min(WIDTH, points)
    early = max(freqs // 2, unit_size)
    later, first = [], early
    while first + unit_size < freqs:
        size = max(unit_size, (freqs - first) // (2 * unit_size) * unit_size)
        later.append((first, size, 0, points))
        first += size
    moved = points // 4
    share = moved // SHARES
    later.append((first, unit_size, 0, points - moved))
    later += [(first, unit_size, points - moved + i * share, share) for i in range(SHARES)]
    batches = early_batches(blocks, points, width)
    groups, low = [], 0
    while low < units:
        groups.append((low, max(1, (units - low) // 2)))
        low += groups[-1][1]
    hbm = pl.BlockSpec(memory_space=pl.ANY)
    bf16 = jnp.bfloat16
    table = ordered_tables(make_table(length, length // 2), n_tm, freqs, early)
    swap = swap_matrix()
    order = swap if rows % GROUP == 0 else order_matrix(unit_size, total, n_space)
    sums = pl.pallas_call(
        functools.partial(kernel, n_tm, n_space, width, early, unit_size, batches, later, groups),
        out_shape=pltpu.VMEM((rows, freqs * 2, total), jnp.float32),
        in_specs=[hbm] * 5,
        out_specs=pl.BlockSpec(memory_space=pltpu.VMEM),
        scratch_shapes=[
            pltpu.VMEM((1, points), jnp.float32),
            pltpu.VMEM(table.shape[1:], bf16),
            pltpu.VMEM(swap.shape, bf16),
            pltpu.VMEM(order.shape, bf16),
            pltpu.VMEM((2, GROUP, length, width), bf16),
            pltpu.VMEM((GROUP, length, width), bf16),
            pltpu.VMEM((n_tm - 1, freqs, 2, blocks, points), bf16),
            pltpu.VMEM((freqs, 2, total, points), bf16),
            pltpu.VMEM((units, n_space, slab, total), bf16),
            pltpu.VMEM((units, n_space - 1, slab, total), bf16),
            pltpu.VMEM((SHARES, n_tm - 1, unit_size, 2, blocks, share), bf16),
            pltpu.VMEM((SHARES, unit_size, 2, total, share), bf16),
            pltpu.SemaphoreType.DMA((4,)),
            pltpu.SemaphoreType.DMA((2, GROUP // PART)),
            pltpu.SemaphoreType.DMA((2,)),
            pltpu.SemaphoreType.DMA((2 + SHARES,)),
            pltpu.SemaphoreType.DMA((len(later),)),
            pltpu.SemaphoreType.DMA((1,)),
            pltpu.SemaphoreType.DMA((len(groups),)),
            pltpu.SemaphoreType.REGULAR((max(n_space // 2 - 1, 1),)),
            pltpu.SemaphoreType.DMA((SHARES,)),
            pltpu.SemaphoreType.DMA((SHARES,)),
            pltpu.SemaphoreType.DMA((SHARES,)),
            pltpu.SemaphoreType.DMA((SHARES,)),
        ],
        compiler_params=pltpu.CompilerParams(
            collective_id=0, has_side_effects=True, vmem_limit_bytes=60 * 1024 * 1024
        ),
    )(
        snapshots,
        weights[None, :],
        table,
        swap,
        order,
    )
    return sums.reshape(rows, freqs, 2, total)


def solution(mesh):
    return jax.shard_map(
        functools.partial(per_device, mesh.shape["tm"], mesh.shape["space"]),
        mesh=mesh,
        in_specs=(P("tm", None, "space"), P("space")),
        out_specs=P("space", "tm", None, None),
        check_vma=False,
    )
```
